512 devices in a mesh: req: 16 (over z), ctx: 32 (over x, y, core).
Axes of the slice: x: 4, y: 4, z: 16, core: 2. Of those that a mesh axis runs over, the one named last changes fastest.
Arguments:
- residual: bfloat16 [64, 7168], P('ctx', 'req'), may hold values from -6 to 6
- query: bfloat16 [64, 128, 576], P('req', 'ctx'), may hold values from -260 to 260
- latent_cache: bfloat16 [32, 16384, 576], P('req', 'ctx'), may hold values from -6 to 6
- lengths: int32 [32], P('req'), may hold values from 4 to 16384, as said below
- w_uv: bfloat16 [128, 512, 128], P('ctx'), may hold values from -6 to 6
- w_o: bfloat16 [16384, 7168], P('ctx', 'req'), may hold values from -0.046875 to 0.046875
- norm_gain: bfloat16 [7168], replicated, may hold values from 0.099609375 to 1.8984375
- routes: int32 [64, 4], replicated, may hold values from 0 to 15, all different within a row; in each aligned block of 64 rows (0 to 63, 64 to 127, ...) at most 32 rows name the same one
- route_weight: float32 [64, 4], replicated, may hold values from 0.2 to 1
- w_gate: bfloat16 [16, 2048, 7168], P('req', 'ctx'), may hold values from -0.0625 to 0.0625
- w_up: bfloat16 [16, 2048, 7168], P('req', 'ctx'), may hold values from -0.0625 to 0.0625
- w_down: bfloat16 [16, 2048, 7168], P('req', 'ctx'), may hold values from -0.125 to 0.125
Outputs:
- layer_out: bfloat16 [64, 7168], P('req', 'ctx')
The draws below stay inside these ranges and needn't reach their ends.
Inputs may be any that keep to these rules, and one draw needn't show every extreme that they name: `lengths`: some request has length exactly 16384. `routes`: each token names 4 different experts; over all 64 tokens no expert is named by more than 32 tokens, a bound that some block reaches.
All inputs are finite; a program needn't handle non-finite values.
Results may differ from the reference program's by a relative error of at most 0.035.
Values may be sent and summed in bfloat16 or wider, within the bound.
A program may use at most 64 MiB of HBM per device.

```python
import math
import jax
import jax.numpy as jnp
import numpy as np
from jax import lax

D = 7168
H = 128
KV_LAT = 512
VD = 128
FF = 2048
EXPERTS = 16
TOP = 4
Q_TOK = 2
CTX_DEV = 512
LATW = 576
HV = 16384
REQUESTS = 32
CONTEXT = 16384
TOKENS = 64
CAP = 32
N_CTX = 32


def draw_latent_cache(key, part):
    base = jnp.clip(jax.random.normal(jax.random.fold_in(key, 12), (REQUESTS, CONTEXT, LATW), jnp.float32), -6.0, 6.0)
    return base.astype(jnp.bfloat16)


def draw_query(key, part):
    base = jnp.clip(jax.random.normal(jax.random.fold_in(key, 13), (TOKENS, H, LATW), jnp.float32), -6.0, 6.0)
    return base.astype(jnp.bfloat16)


def draw_lengths(key, part):
    drawn = jax.random.randint(jax.random.fold_in(key, 16), (REQUESTS,), 4, CONTEXT + 1)
    longest = jax.random.randint(jax.random.fold_in(key, 17), (), 0, REQUESTS)
    return jnp.where(jnp.arange(REQUESTS, dtype=jnp.int32) == longest, CONTEXT, drawn).astype(jnp.int32)


def steps_of(key, extent, pieces, low, high):
    loudness = 1.0
    for axis_at, blocks in pieces:
        heights = jax.random.uniform(jax.random.fold_in(jax.random.fold_in(key, 6), axis_at), (blocks,), jnp.float32, low / len(pieces), high / len(pieces))
        loudness = loudness * jnp.repeat(jnp.exp(heights), extent[axis_at] // blocks).reshape((-1,) + (1,) * (len(extent) - 1 - axis_at))
    return loudness


def shared_out(rng, own, number, rows, number_of, top, most, lean):
    order = jax.random.permutation(rng, number_of)
    heavy_load, usual = portions_of(number_of, rows * top, most, lean, True), portions_of(number_of, rows * top, most, lean, False)
    places = jnp.arange(number_of)

    def named(tallies, rotation):
        used = int((tallies > 0).sum())
        fixed = max(1, used // 4)
        moved = fixed + (places - fixed + rotation * (used - fixed)) % max(1, number_of - fixed)
        return jnp.zeros((number_of,), jnp.int32).at[order[jnp.where(places < fixed, places, moved)]].set(jnp.asarray(tallies, jnp.int32))

    tallies = jnp.where(number % 4 == 0, named(heavy_load, number // 4), named(usual, number - number // 4 - 1))
    mixed = jax.random.permutation(jax.random.fold_in(own, 3), number_of)
    donor, taker = mixed[0:number_of // 2 * 2:2], mixed[1:number_of // 2 * 2:2]
    room = jnp.minimum(tallies[donor] - 1, most - tallies[taker]) // 2
    room = jnp.where((donor == order[0]) | (taker == order[0]) | (tallies[taker] == 0), 0, jnp.maximum(room, 0))
    moved = jax.random.randint(jax.random.fold_in(own, 4), (number_of // 2,), 0, 1 << 20) % (room + 1)
    tallies = tallies.at[donor].add(-moved).at[taker].add(moved)
    members = jnp.searchsorted(jnp.cumsum(tallies), jnp.arange(rows * top), side="right").astype(jnp.int32)
    table = members.reshape(top, rows).T
    table = table[jax.random.permutation(jax.random.fold_in(own, 1), rows)]
    rotation = jax.random.randint(jax.random.fold_in(own, 2), (rows, 1), 0, top)
    return jnp.take_along_axis(table, (jnp.arange(top)[None, :] + rotation) % top, axis=1)


def portions_of(number_of, total, most, lean, full):
    weights = [(1 << 20) // math.isqrt(rank ** lean) + 1 for rank in range(1, number_of + 1)]
    largest = most if full else min(most, max(-(-total // number_of), total * weights[0] // sum(weights)))
    least = 1 if total - largest >= number_of - 1 else 0
    given, spare = [largest] + [least] * (number_of - 1), total - largest - least * (number_of - 1)
    while spare > 0:
        free = [i for i in range(1, number_of) if given[i] < largest] or [i for i in range(1, number_of) if given[i] < most]
        mass, budget = sum([weights[i] for i in free]), spare
        for i in free:
            extra = min(most - given[i], max(1, budget * weights[i] // mass), spare)
            given[i] = given[i] + extra
            spare = spare - extra
    return np.array(given)


def scatter_about(stream_key, dims, scale, reach, pieces=(), kind=jnp.bfloat16):
    result = jax.random.normal(stream_key, dims, jnp.float32) * scale
    if len(pieces) > 0:
        result = steps_of(stream_key, dims, pieces, -0.22, 0.18) * result
    return jnp.clip(result, min=-reach, max=reach).astype(kind)


def setup_inputs(seed: int = 0) -> dict:
    key_of = jax.random.split(jax.random.key(seed), 13)
    residual = scatter_about(key_of[0], (TOKENS, D), 1.0, 6.0, ((0, 32), (1, 16)))
    query = draw_query(jax.random.fold_in(key_of[12], 71), 0)
    latent_cache = draw_latent_cache(jax.random.fold_in(key_of[12], 71), 0)
    lengths = draw_lengths(jax.random.fold_in(key_of[12], 71), 0)
    w_uv = scatter_about(key_of[4], (H, KV_LAT, VD), 0.4, 6.0, ((0, 32),))
    w_o = scatter_about(key_of[5], (HV, D), HV ** -0.5, 0.046875, ((0, 32), (1, 16)))
    norm_gain = jnp.clip(1.0 + 0.18 * jax.random.normal(key_of[6], (D,), jnp.float32), 0.099609375, 1.8984375).astype(jnp.bfloat16)
    routes_keys = jax.random.split(jax.random.fold_in(key_of[7], 1), TOKENS // TOKENS)
    routes_turns = jax.random.permutation(jax.random.fold_in(key_of[7], 3), TOKENS // TOKENS)
    routes = jax.vmap(lambda own, number: shared_out(jax.random.fold_in(key_of[7], 2), own, number, TOKENS, EXPERTS, TOP, CAP, 1))(routes_keys, routes_turns).reshape((TOKENS, TOP))
    route_weight = jnp.clip(jax.random.uniform(key_of[8], (TOKENS, TOP), jnp.float32, 0.2, 1.0), 0.2, 1.0)
    w_gate = scatter_about(key_of[9], (EXPERTS, FF, D), D ** -0.5, 0.0625, ((0, 16), (1, 32)))
    w_up = scatter_about(key_of[10], (EXPERTS, FF, D), D ** -0.5, 0.0625, ((0, 16), (1, 32)))
    w_down = scatter_about(key_of[11], (EXPERTS, FF, D), FF ** -0.5, 0.125, ((0, 16), (1, 32)))
    return {"residual": residual, "query": query, "latent_cache": latent_cache, "lengths": lengths, "w_uv": w_uv, "w_o": w_o, "norm_gain": norm_gain, "routes": routes, "route_weight": route_weight, "w_gate": w_gate, "w_up": w_up, "w_down": w_down}


SOFTMAX_SCALE = 192.0 ** (-0.5)
NEG_FILL = -1e+30
NORM_EPS = 1e-06

def local_softmax(scores, visible, values):
    masked = jnp.where(visible, scores, -jnp.inf)
    peaks = lax.optimization_barrier(jnp.max(masked, axis=-1))
    peaks = jnp.where(jnp.any(visible, axis=-1), peaks, jnp.zeros_like(peaks))
    raised = jnp.exp(masked - peaks[..., None])
    totals = lax.optimization_barrier(jnp.sum(raised, axis=-1))
    probs = lax.optimization_barrier(raised.astype(jnp.bfloat16)).astype(jnp.float32)
    mixed = jnp.einsum('rqp,rpd->rqd', probs, values, precision=lax.Precision.HIGHEST)
    filled = totals > 0.0
    safe_totals = jnp.where(filled, totals, jnp.ones_like(totals))
    shard_out = jnp.where(filled[..., None], mixed / safe_totals[..., None], jnp.zeros_like(mixed)).astype(jnp.bfloat16)
    shard_log = jnp.where(filled, peaks + jnp.log(safe_totals), jnp.full_like(peaks, NEG_FILL))
    return (shard_out, shard_log)

def reference(residual, query, latent_cache, lengths, w_uv, w_o, norm_gain, routes, route_weight, w_gate, w_up, w_down):
    grouped = query.reshape(REQUESTS, Q_TOK * H, LATW).astype(jnp.float32)
    shards = latent_cache.reshape(REQUESTS, N_CTX, CTX_DEV, LATW)
    offsets = jnp.arange(Q_TOK * H, dtype=jnp.int32) // H
    limits = lengths[:, None] - Q_TOK + offsets[None, :]

    def one_shard(index):
        block = lax.dynamic_index_in_dim(shards, index, 1, keepdims=False).astype(jnp.float32)
        scores = jnp.einsum('rqd,rpd->rqp', grouped, block, precision=lax.Precision.HIGHEST) * SOFTMAX_SCALE
        positions = index * CTX_DEV + jnp.arange(CTX_DEV, dtype=jnp.int32)
        visible = positions[None, None, :] <= limits[:, :, None]
        return local_softmax(scores, visible, block[:, :, :KV_LAT])
    parts, logs = lax.map(one_shard, jnp.arange(N_CTX, dtype=jnp.int32))
    top_log = lax.optimization_barrier(jnp.max(logs, axis=0))
    factors = jnp.exp(logs - top_log[None])
    numer = lax.optimization_barrier(jnp.sum(factors[..., None] * parts.astype(jnp.float32), axis=0))
    denom = lax.optimization_barrier(jnp.sum(factors, axis=0))
    latent = (numer / denom[..., None]).astype(jnp.bfloat16).reshape(TOKENS, H, KV_LAT)
    projected = jnp.einsum('thd,hde->the', latent.astype(jnp.float32), w_uv.astype(jnp.float32), precision=lax.Precision.HIGHEST)
    head_value = projected.astype(jnp.bfloat16).reshape(TOKENS, HV)
    attention = jnp.dot(head_value, w_o, preferred_element_type=jnp.float32)
    mid = (residual.astype(jnp.float32) + attention).astype(jnp.bfloat16)
    widened = mid.astype(jnp.float32)
    scale_rows = lax.rsqrt(lax.optimization_barrier(jnp.mean(widened * widened, axis=-1, keepdims=True)) + NORM_EPS)
    normed = (widened * scale_rows * norm_gain.astype(jnp.float32)).astype(jnp.bfloat16)
    expert_ids = jnp.arange(EXPERTS, dtype=jnp.int32)
    coefs = lax.optimization_barrier(jnp.sum(jnp.where(routes[:, :, None] == expert_ids[None, None, :], route_weight[:, :, None], jnp.zeros_like(route_weight)[:, :, None]), axis=1))

    def expert_step(carry, items):
        gate_w, up_w, down_w, coef = items
        gate_vals = jnp.dot(normed, gate_w.T, preferred_element_type=jnp.float32)
        up_vals = jnp.dot(normed, up_w.T, preferred_element_type=jnp.float32)
        hidden = (jax.nn.silu(gate_vals) * up_vals * coef[:, None]).astype(jnp.bfloat16)
        return (carry + jnp.dot(hidden, down_w, preferred_element_type=jnp.float32), None)
    moe_out, _ = lax.scan(expert_step, jnp.zeros((TOKENS, D), jnp.float32), (w_gate, w_up, w_down, coefs.T))
    return (mid.astype(jnp.float32) + moe_out).astype(jnp.bfloat16)
```

```python
import functools

import jax
import jax.numpy as jnp
from jax import lax
from jax.experimental import pallas as pl
from jax.experimental.pallas import tpu as pltpu
from jax.sharding import PartitionSpec as P

MESH = pl.DeviceIdType.MESH
SCALE = 192.0 ** (-0.5)
NEG = -1e30
EPS = 1e-06
BF = jnp.bfloat16
F32 = jnp.float32
NZ = 16
NC = 32
NCHIP = 16
FAR = (10, 2, 8, 9, 11, 6, 14, 1, 3, 4, 12, 5, 7, 13, 15)
ZFAR = (8, 7, 9, 6, 10, 5, 11, 4, 12, 3, 13, 2, 14, 1, 15)


def dot(a, b):
    return jnp.dot(a, b, preferred_element_type=F32)


def dot_t(a, b):
    return lax.dot_general(a, b, (((1,), (1,)), ((), ())), preferred_element_type=F32)


def iota(shape, axis):
    return lax.broadcasted_iota(jnp.int32, shape, axis)


def body(
    lens, q_hbm, cache_hbm, wuv_hbm, wo_hbm, res_hbm, gain_ref, routes_ref, rw_ref,
    wg_hbm, wu_hbm, wd_hbm,
    out_ref,
    qin, cbuf, wuv, wo, res, gu, wd,
    qs, qbuf, osend, obuf, vs, vbuf, fs, fbuf, gs, gbuf, mid8, xs, xbuf, isend, ibuf, js, jbuf,
    loc, sib_s, sib_r, snd, rcv,
):
    z = lax.axis_index("req")
    c = lax.axis_index("ctx")
    core = lax.rem(c, 2)
    chip = c // 2
    sib = c + 1 - 2 * core

    def chip_at(s):
        x = lax.rem(chip // 4 + s // 4, 4)
        y = lax.rem(lax.rem(chip, 4) + s % 4, 4)
        return x * 4 + y

    def back(s):
        return ((4 - s // 4) % 4) * 4 + (4 - s % 4) % 4

    locals_ = [
        pltpu.make_async_copy(q_hbm, qin, loc.at[0]),
        pltpu.make_async_copy(cache_hbm, cbuf.at[0], loc.at[1]),
        pltpu.make_async_copy(wuv_hbm, wuv, loc.at[2]),
        pltpu.make_async_copy(wo_hbm, wo, loc.at[3]),
        pltpu.make_async_copy(res_hbm, res, loc.at[4]),
        pltpu.make_async_copy(wg_hbm.at[0], gu.at[pl.ds(0, 64)], loc.at[5]),
        pltpu.make_async_copy(wu_hbm.at[0], gu.at[pl.ds(128, 64)], loc.at[6]),
        pltpu.make_async_copy(wd_hbm.at[0], wd.at[pl.ds(0, 64)], loc.at[7]),
    ]
    for copy in locals_:
        copy.start()

    barrier = pltpu.get_barrier_semaphore()

    @pl.loop(1, NC)
    def _(s):
        pl.semaphore_signal(
            barrier, inc=1, device_id=(z, lax.rem(c + s, NC)), device_id_type=MESH
        )

    @pl.loop(1, NZ)
    def _(s):
        pl.semaphore_signal(
            barrier, inc=1, device_id=(lax.rem(z + s, NZ), c), device_id_type=MESH
        )

    pl.semaphore_wait(barrier, NC + NZ - 2)

    def remote(src, dst, send, recv, dev):
        return pltpu.make_async_remote_copy(
            src_ref=src, dst_ref=dst, send_sem=send, recv_sem=recv,
            device_id=dev, device_id_type=MESH,
        )

    def drain(ref, sem):
        pltpu.make_async_copy(ref, ref, sem).wait()

    twins = [
        remote(cache_hbm, cbuf.at[1], sib_s.at[0], sib_r.at[0], (z, sib)),
        remote(wg_hbm.at[0], gu.at[pl.ds(64, 64)], sib_s.at[1], sib_r.at[1], (z, sib)),
        remote(wu_hbm.at[0], gu.at[pl.ds(192, 64)], sib_s.at[2], sib_r.at[2], (z, sib)),
        remote(wd_hbm.at[0], wd.at[pl.ds(64, 64)], sib_s.at[3], sib_r.at[3], (z, sib)),
    ]
    twins[0].start()

    locals_[0].wait()
    for r in range(2):
        rows = jnp.concatenate(
            [qin[2 * r].astype(F32), qin[2 * r + 1].astype(F32)], axis=0
        ).astype(BF)
        qs[r] = rows
        qbuf[0, r] = rows
    for s in FAR:
        remote(
            qs, qbuf.at[back(s)], snd.at[0], rcv.at[0], (z, chip_at(s) * 2 + core)
        ).start()
    for copy in twins[1:]:
        copy.start()

    locals_[1].wait()
    twins[0].wait_recv()
    drain(qbuf.at[pl.ds(1, 15)], rcv.at[0])
    row_k = lax.rem(iota((128, 512), 0) // 4, 2)
    lane_p = iota((128, 512), 1)
    lane_e = iota((128, 128), 1)
    for r in range(2):
        ql = qbuf[:, r].astype(F32).reshape(128, 576).astype(BF)
        limit = lens[r] - 2 + row_k
        see0 = (c * 512 + lane_p) <= limit
        see1 = (sib * 512 + lane_p) <= limit
        s0 = jnp.where(see0, dot_t(ql, cbuf[0, r]) * SCALE, NEG)
        s1 = jnp.where(see1, dot_t(ql, cbuf[1, r]) * SCALE, NEG)
        peak = jnp.maximum(
            jnp.max(s0, axis=1, keepdims=True), jnp.max(s1, axis=1, keepdims=True)
        )
        peak = jnp.where(peak > 0.5 * NEG, peak, 0.0)
        e0 = jnp.exp(s0 - peak)
        e1 = jnp.exp(s1 - peak)
        total = jnp.sum(e0, axis=1, keepdims=True) + jnp.sum(e1, axis=1, keepdims=True)
        mixed = dot(e0.astype(BF), cbuf[0, r, :, :512]) + dot(
            e1.astype(BF), cbuf[1, r, :, :512]
        )
        filled = total > 0.0
        safe = jnp.where(filled, total, 1.0)
        part = jnp.where(filled, mixed / safe, 0.0)
        log = jnp.where(filled, peak + jnp.log(safe), NEG)
        hi = log.astype(BF).astype(F32)
        mi = (log - hi).astype(BF).astype(F32)
        lo = log - hi - mi
        tail = jnp.where(
            lane_e == 0, hi, jnp.where(lane_e == 1, mi, jnp.where(lane_e == 2, lo, 0.0))
        )
        osend[:, r, :, :512] = part.reshape(16, 8, 512).astype(BF)
        osend[:, r, :, 512:] = tail.reshape(16, 8, 128).astype(BF)
    for s in FAR:
        remote(
            osend.at[s], obuf.at[back(s)], snd.at[1], rcv.at[1],
            (z, chip_at(s) * 2 + core),
        ).start()
    obuf[0] = osend[0]

    locals_[2].wait()
    drain(obuf.at[pl.ds(1, 15)], rcv.at[1])
    latents = []
    for r in range(2):
        logs = jnp.sum(obuf[:, r, :, 512:].astype(F32), axis=2, keepdims=True)
        top = jnp.max(logs, axis=0, keepdims=True)
        factor = jnp.exp(logs - top)
        numer = jnp.sum(factor * obuf[:, r, :, :512].astype(F32), axis=0)
        latents.append(numer / jnp.sum(factor, axis=0))
    latent = jnp.concatenate(latents, axis=0).astype(BF)
    r8, c16 = iota((8, 16), 0), iota((8, 16), 1)
    halves = [None, None]
    for h in range(4):
        pick = (r8 // 4 == h // 2) & (c16 == 4 * lax.rem(r8, 4) + h)
        rows = dot(jnp.where(pick, 1.0, 0.0).astype(BF), latent).astype(BF)
        val = dot(rows, wuv[h])
        halves[h % 2] = val if halves[h % 2] is None else halves[h % 2] + val
    vrow = jnp.concatenate(halves, axis=1).astype(BF)
    vs[...] = vrow
    for s in ZFAR:
        remote(
            vs, vbuf.at[z], snd.at[2], rcv.at[2], (lax.rem(z + s, NZ), c)
        ).start()
    vbuf[z] = vrow

    locals_[3].wait()
    drain(vbuf.at[pl.ds(0, 15)], rcv.at[2])
    vals = vbuf[...].astype(F32).reshape(128, 256).astype(BF)
    y0 = dot(vals, wo[:256])
    y1 = dot(vals, wo[256:])
    y = (y0 + pltpu.roll(y1, 124, 0)).reshape(16, 8, 448)
    fs[:, 0] = y[:, 0:2]
    fs[:, 1] = y[:, 2:4]
    for s in FAR:
        for k in range(2):
            dst = chip_at(s)
            remote(
                fs.at[dst, k], fbuf.at[c], snd.at[3], rcv.at[3], (z, dst * 2 + k)
            ).start()
    remote(fs.at[chip, 1 - core], fbuf.at[c], snd.at[3], rcv.at[3], (z, sib)).start()
    fbuf[c] = fs[chip, core]

    locals_[4].wait()
    drain(fbuf.at[pl.ds(0, 31)], rcv.at[3])
    mid = (jnp.sum(fbuf[...], axis=0) + res[...].astype(F32)).astype(BF).astype(F32)
    gs[...] = mid
    for s in ZFAR:
        remote(
            gs, gbuf.at[z], snd.at[4], rcv.at[4], (lax.rem(z + s, NZ), c)
        ).start()
    gbuf[z] = mid

    drain(gbuf.at[pl.ds(0, 15)], rcv.at[4])
    for i in range(NZ):
        q, j = i // 4, i % 4
        mid8[2 * q : 2 * q + 2, 448 * j : 448 * j + 448] = gbuf[i]
    m = mid8[...]
    sq = jnp.sum(m * m, axis=1, keepdims=True)
    sq = sq + pltpu.roll(sq, 2, 0)
    sq = sq + pltpu.roll(sq, 4, 0)
    norm = (m * lax.rsqrt(sq * (1.0 / 7168.0) + EPS) * gain_ref[...]).astype(BF)
    xs[...] = norm
    for s in FAR:
        remote(
            xs, xbuf.at[chip], snd.at[5], rcv.at[5], (z, chip_at(s) * 2 + core)
        ).start()
    xbuf[chip] = norm
    r8w = iota((8, 1792), 0)
    for q in range(4):
        rows = m if q == 0 else pltpu.roll(m, 8 - 2 * q, 0)
        rows = jnp.where(r8w < 2, rows, 0.0)
        wd[128:144, 1792 * q : 1792 * (q + 1)] = jnp.concatenate(
            [rows, jnp.zeros_like(rows)], axis=0
        ).astype(BF)

    match = routes_ref[...] == z
    coef = jnp.sum(jnp.where(match, rw_ref[...], 0.0), axis=1, keepdims=True)
    coef = jnp.broadcast_to(coef, (64, 128))
    row = iota((128, 64), 0)
    token = 4 * (row // 8) + 2 * core + lax.rem(row, 2)
    pick = jnp.where((token == iota((128, 64), 1)) & (lax.rem(row, 8) < 2), 1.0, 0.0)
    coefs = jnp.dot(
        pick, coef, preferred_element_type=F32, precision=lax.Precision.HIGHEST
    )

    locals_[5].wait()
    locals_[6].wait()
    locals_[7].wait()
    for copy in twins[1:]:
        copy.wait_recv()
    drain(xbuf.at[pl.ds(0, 15)], rcv.at[5])
    x = xbuf[...].astype(F32).reshape(128, 1792).astype(BF)
    row_q = lax.rem(iota((128, 256), 0), 8) // 2
    both = jnp.zeros((128, 256), F32)
    for q in range(4):
        part = dot_t(x, gu[:, 1792 * q : 1792 * (q + 1)])
        both = both + jnp.where(row_q == q, part, 0.0)
    both = both + pltpu.roll(both, 126, 0)
    both = both + pltpu.roll(both, 124, 0)
    gate, up = both[:, :128], both[:, 128:]
    hidden = gate / (1.0 + jnp.exp(-gate)) * up * coefs
    keep = lax.rem(iota((128, 128), 0), 8) < 2
    hidden = jnp.where(keep, hidden, 0.0).astype(BF)
    r32, c128 = iota((32, 128), 0), iota((32, 128), 1)
    squeeze = jnp.where(c128 == 8 * (r32 // 2) + lax.rem(r32, 2), 1.0, 0.0).astype(BF)
    short = dot(squeeze, hidden).astype(BF)
    r32s, c16s = iota((32, 16), 0), iota((32, 16), 1)
    own = (r32s // 2 == chip) & (chip == z) & (c16s == lax.rem(r32s, 2))
    short = jnp.concatenate([short, jnp.where(own, 1.0, 0.0).astype(BF)], axis=1)
    for q in range(4):
        o = dot(short, wd[:, 1792 * q : 1792 * (q + 1)])
        for d in range(8):
            isend[8 * q + d] = o[:, 224 * d : 224 * d + 224].astype(BF)
    for s in FAR:
        for k in range(2):
            dst = chip_at(s) * 2 + k
            remote(
                isend.at[dst], ibuf.at[c], snd.at[6], rcv.at[6], (z, dst)
            ).start()
    remote(isend.at[sib], ibuf.at[c], snd.at[6], rcv.at[6], (z, sib)).start()
    ibuf[c] = isend[c]

    drain(ibuf.at[pl.ds(0, 31)], rcv.at[6])
    for k in range(2):
        acc = ibuf[k].astype(F32)
        for i in range(1, 16):
            acc = acc + ibuf[2 * i + k].astype(F32)
        for p in range(NZ):
            js[p, 2 * k : 2 * k + 2, :] = acc[2 * p : 2 * p + 2]
    for s in ZFAR:
        dst = lax.rem(z + s, NZ)
        remote(js.at[dst], jbuf.at[z], snd.at[7], rcv.at[7], (dst, c)).start()
    jbuf[z] = js[z]
    drain(jbuf.at[pl.ds(0, 15)], rcv.at[7])
    out_ref[...] = jnp.sum(jbuf[...], axis=0).astype(BF)

    for copy in twins:
        copy.wait_send()
    drain(qbuf.at[pl.ds(0, 15)], snd.at[0])
    drain(obuf.at[pl.ds(0, 15)], snd.at[1])
    drain(vbuf.at[pl.ds(0, 15)], snd.at[2])
    drain(fbuf.at[pl.ds(0, 31)], snd.at[3])
    drain(gbuf.at[pl.ds(0, 15)], snd.at[4])
    drain(xbuf.at[pl.ds(0, 15)], snd.at[5])
    drain(ibuf.at[pl.ds(0, 31)], snd.at[6])
    drain(jbuf.at[pl.ds(0, 15)], snd.at[7])


def local(
    residual, query, latent_cache, lengths, w_uv, w_o, norm_gain, routes, route_weight,
    w_gate, w_up, w_down,
):
    gain8 = jnp.repeat(norm_gain.reshape(4, 1792).astype(F32), 2, axis=0)
    hbm = pl.BlockSpec(memory_space=pl.ANY)
    vmem = pl.BlockSpec(memory_space=pltpu.VMEM)
    smem = pl.BlockSpec(memory_space=pltpu.SMEM)
    V = pltpu.VMEM
    D = pltpu.SemaphoreType.DMA
    return pl.pallas_call(
        body,
        out_shape=jax.ShapeDtypeStruct((4, 224), BF),
        in_specs=[smem, hbm, hbm, hbm, hbm, hbm, vmem, vmem, vmem, hbm, hbm, hbm],
        out_specs=vmem,
        scratch_shapes=[
            V((4, 4, 576), BF),
            V((2, 2, 512, 576), BF),
            V((4, 512, 128), BF),
            V((512, 448), BF),
            V((2, 448), BF),
            V((256, 7168), BF),
            V((144, 7168), BF),
            V((2, 8, 576), BF),
            V((16, 2, 8, 576), BF),
            V((16, 2, 8, 640), BF),
            V((16, 2, 8, 640), BF),
            V((8, 256), BF),
            V((16, 8, 256), BF),
            V((16, 2, 2, 448), F32),
            V((32, 2, 448), F32),
            V((2, 448), F32),
            V((16, 2, 448), F32),
            V((8, 1792), F32),
            V((8, 1792), BF),
            V((16, 8, 1792), BF),
            V((32, 32, 224), BF),
            V((32, 32, 224), BF),
            V((16, 4, 224), F32),
            V((16, 4, 224), F32),
            D((8,)),
            D((4,)),
            D((4,)),
            D((8,)),
            D((8,)),
        ],
        compiler_params=pltpu.CompilerParams(
            collective_id=0, has_side_effects=True, vmem_limit_bytes=48 << 20
        ),
        name="decode_layer",
    )(
        lengths, query, latent_cache, w_uv, w_o, residual, gain8, routes, route_weight,
        w_gate, w_up, w_down,
    )


def solution(mesh):
    in_specs = (
        P("ctx", "req"),
        P("req", "ctx", None),
        P("req", "ctx", None),
        P("req"),
        P("ctx", None, None),
        P("ctx", "req"),
        P(),
        P(),
        P(),
        P("req", "ctx", None),
        P("req", "ctx", None),
        P("req", "ctx", None),
    )
    return jax.shard_map(
        local, mesh=mesh, in_specs=in_specs, out_specs=P("req", "ctx"), check_vma=False
    )
```

```python
import jax
import jax.numpy as jnp
from jax import lax
from jax.experimental import pallas as pl
from jax.experimental.pallas import tpu as pltpu
from jax.sharding import PartitionSpec as P

MESH = pl.DeviceIdType.MESH
SCALE = 192.0 ** (-0.5)
NEG = -1e30
EPS = 1e-06
BF = jnp.bfloat16
F32 = jnp.float32
NZ = 16
NC = 32
NCHIP = 16
FAR = (10, 2, 8, 9, 11, 6, 14, 1, 3, 4, 12, 5, 7, 13, 15)
ZFAR = (8, 7, 9, 6, 10, 5, 11, 4, 12, 3, 13, 2, 14, 1, 15)


def dot(a, b):
    return jnp.dot(a, b, preferred_element_type=F32)


def dot_t(a, b):
    return lax.dot_general(a, b, (((1,), (1,)), ((), ())), preferred_element_type=F32)


def iota(shape, axis):
    return lax.broadcasted_iota(jnp.int32, shape, axis)


def body(
    lens, q_hbm, cache_hbm, wuv_hbm, wo_hbm, res_hbm, gain_hbm, routes_hbm, rw_hbm,
    wg_hbm, wu_hbm, wd_hbm,
    out_ref,
    qin, cbuf, wuv, wo, res, gain, routes, rw, gain8, gu, wd,
    qs, qbuf, osend, obuf, vs, vbuf, fs, fbuf, gs, gbuf, mid8, xs, xbuf, isend, ibuf, js, jbuf,
    loc, sib_s, sib_r, snd, rcv,
):
    z = lax.axis_index("req")
    c = lax.axis_index("ctx")
    core = lax.rem(c, 2)
    chip = c // 2
    sib = c + 1 - 2 * core

    def chip_at(s):
        x = lax.rem(chip // 4 + s // 4, 4)
        y = lax.rem(lax.rem(chip, 4) + s % 4, 4)
        return x * 4 + y

    def back(s):
        return ((4 - s // 4) % 4) * 4 + (4 - s % 4) % 4

    todo = {}

    def begin(name, copy):
        copy.start()
        todo[name] = copy.wait

    def wait(*names):
        for name in names:
            todo.pop(name)()

    def drain(ref, sem):
        pltpu.make_async_copy(ref, ref, sem).wait()

    own, other = pl.ds(0, 512), pl.ds(512, 512)
    for i, (name, src, dst) in enumerate((
        ("q", q_hbm, qin),
        ("cache", cache_hbm, cbuf.at[:, :, own]),
        ("gain", gain_hbm, gain),
        ("routes", routes_hbm, routes),
        ("rw", rw_hbm, rw),
        ("res", res_hbm, res),
        ("wuv", wuv_hbm, wuv),
        ("wo", wo_hbm, wo),
        ("wg", wg_hbm.at[0], gu.at[pl.ds(0, 64)]),
        ("wu", wu_hbm.at[0], gu.at[pl.ds(128, 64)]),
        ("wd", wd_hbm.at[0], wd.at[pl.ds(0, 64)]),
    )):
        begin(name, pltpu.make_async_copy(src, dst, loc.at[i]))

    barrier = pltpu.get_barrier_semaphore()

    @pl.loop(1, NC)
    def _(s):
        pl.semaphore_signal(
            barrier, inc=1, device_id=(z, lax.rem(c + s, NC)), device_id_type=MESH
        )

    @pl.loop(1, NZ)
    def _(s):
        pl.semaphore_signal(
            barrier, inc=1, device_id=(lax.rem(z + s, NZ), c), device_id_type=MESH
        )

    pl.semaphore_wait(barrier, NC + NZ - 2)

    def remote(src, dst, send, recv, dev):
        return pltpu.make_async_remote_copy(
            src_ref=src, dst_ref=dst, send_sem=send, recv_sem=recv,
            device_id=dev, device_id_type=MESH,
        )

    def twin(i, name, src, dst):
        copy = remote(src, dst, sib_s.at[i], sib_r.at[i], (z, sib))
        copy.start()
        todo[name] = copy.wait_recv
        todo[name + "_sent"] = copy.wait_send

    def sent(i, ref):
        todo["sent%d" % i] = lambda: drain(ref, snd.at[i])

    wait("q")
    for r in range(2):
        rows = jnp.concatenate(
            [qin[2 * r].astype(F32), qin[2 * r + 1].astype(F32)], axis=0
        ).astype(BF)
        qs[r] = rows
        qbuf[0, r] = rows
    twin(0, "cache2", cache_hbm, cbuf.at[:, :, other])
    for s in FAR:
        remote(
            qs, qbuf.at[back(s)], snd.at[0], rcv.at[0], (z, chip_at(s) * 2 + core)
        ).start()
    sent(0, qbuf.at[pl.ds(0, 15)])
    twin(1, "wg2", wg_hbm.at[0], gu.at[pl.ds(64, 64)])
    twin(2, "wu2", wu_hbm.at[0], gu.at[pl.ds(192, 64)])
    twin(3, "wd2", wd_hbm.at[0], wd.at[pl.ds(64, 64)])

    wait("gain", "routes", "rw")
    g = gain[...].astype(F32)
    for i in range(56):
        q, j = i // 14, i % 14
        gain8[2 * q : 2 * q + 2, 128 * j : 128 * j + 128] = jnp.broadcast_to(
            g[i : i + 1], (2, 128)
        )
    coef = jnp.sum(jnp.where(routes[...] == z, rw[...], 0.0), axis=0, keepdims=True)
    row = iota((128, 64), 0)
    token = 4 * (row // 8) + 2 * core + lax.rem(row, 2)
    pick = (token == iota((128, 64), 1)) & (lax.rem(row, 8) < 2)
    coefs = jnp.sum(jnp.where(pick, coef, 0.0), axis=1, keepdims=True)

    wait("cache", "cache2")
    drain(qbuf.at[pl.ds(1, 15)], rcv.at[0])
    row_k = lax.rem(iota((128, 1024), 0) // 4, 2)
    lane_p = iota((128, 1024), 1)
    place = jnp.where(lane_p < 512, c * 512 + lane_p, sib * 512 + lane_p - 512)
    lane_e = iota((128, 128), 1)
    for r in range(2):
        ql = qbuf[:, r].astype(F32).reshape(128, 576).astype(BF)
        see = place <= lens[r] - 2 + row_k
        score = jnp.where(see, dot(ql, cbuf[r]) * SCALE, NEG)
        peak = jnp.max(score, axis=1, keepdims=True)
        peak = jnp.where(peak > 0.5 * NEG, peak, 0.0)
        raised = jnp.exp(score - peak)
        total = jnp.sum(raised, axis=1, keepdims=True)
        mixed = dot_t(raised.astype(BF), cbuf[r, :512])
        filled = total > 0.0
        safe = jnp.where(filled, total, 1.0)
        part = jnp.where(filled, mixed / safe, 0.0)
        log = jnp.where(filled, peak + jnp.log(safe), NEG)
        hi = log.astype(BF).astype(F32)
        mi = (log - hi).astype(BF).astype(F32)
        lo = log - hi - mi
        tail = jnp.where(
            lane_e == 0, hi, jnp.where(lane_e == 1, mi, jnp.where(lane_e == 2, lo, 0.0))
        )
        osend[r, :, :, :512] = part.reshape(16, 8, 512).astype(BF)
        osend[r, :, :, 512:] = tail.reshape(16, 8, 128).astype(BF)
        for s in FAR:
            remote(
                osend.at[r, s], obuf.at[r, back(s)], snd.at[1 + r], rcv.at[1 + r],
                (z, chip_at(s) * 2 + core),
            ).start()
        obuf[r, 0] = osend[r, 0]
        sent(1 + r, obuf.at[r, pl.ds(0, 15)])

    wait("wuv")
    latents = []
    for r in range(2):
        drain(obuf.at[r, pl.ds(1, 15)], rcv.at[1 + r])
        logs = jnp.sum(obuf[r, :, :, 512:].astype(F32), axis=2, keepdims=True)
        top = jnp.max(logs, axis=0, keepdims=True)
        factor = jnp.exp(logs - top)
        numer = jnp.sum(factor * obuf[r, :, :, :512].astype(F32), axis=0)
        latents.append(numer / jnp.sum(factor, axis=0))
    latent = jnp.concatenate(latents, axis=0).astype(BF)
    r8, c16 = iota((8, 16), 0), iota((8, 16), 1)
    halves = [None, None]
    for h in range(4):
        pick = (r8 // 4 == h // 2) & (c16 == 4 * lax.rem(r8, 4) + h)
        rows = dot(jnp.where(pick, 1.0, 0.0).astype(BF), latent).astype(BF)
        val = dot(rows, wuv[h])
        halves[h % 2] = val if halves[h % 2] is None else halves[h % 2] + val
    vrow = jnp.concatenate(halves, axis=1).astype(BF)
    vs[...] = vrow
    for s in ZFAR:
        remote(
            vs, vbuf.at[z], snd.at[3], rcv.at[3], (lax.rem(z + s, NZ), c)
        ).start()
    vbuf[z] = vrow
    sent(3, vbuf.at[pl.ds(0, 15)])

    wait("wo")
    drain(vbuf.at[pl.ds(0, 15)], rcv.at[3])
    vals = vbuf[...].astype(F32).reshape(128, 256).astype(BF)
    y0 = dot_t(vals, wo[:, :256])
    y1 = dot_t(vals, wo[:, 256:])
    y = (y0 + pltpu.roll(y1, 124, 0)).reshape(16, 8, 448)
    fs[:, 0] = y[:, 0:2]
    fs[:, 1] = y[:, 2:4]
    for s in FAR:
        for k in range(2):
            dst = chip_at(s)
            remote(
                fs.at[dst, k], fbuf.at[c], snd.at[4], rcv.at[4], (z, dst * 2 + k)
            ).start()
    remote(fs.at[chip, 1 - core], fbuf.at[c], snd.at[4], rcv.at[4], (z, sib)).start()
    fbuf[c] = fs[chip, core]
    sent(4, fbuf.at[pl.ds(0, 31)])

    wait("res")
    drain(fbuf.at[pl.ds(0, 31)], rcv.at[4])
    mid = (jnp.sum(fbuf[...], axis=0) + res[...].astype(F32)).astype(BF).astype(F32)
    gs[...] = mid
    for s in ZFAR:
        remote(
            gs, gbuf.at[z], snd.at[5], rcv.at[5], (lax.rem(z + s, NZ), c)
        ).start()
    gbuf[z] = mid
    sent(5, gbuf.at[pl.ds(0, 15)])

    drain(gbuf.at[pl.ds(0, 15)], rcv.at[5])
    for i in range(NZ):
        q, j = i // 4, i % 4
        mid8[2 * q : 2 * q + 2, 448 * j : 448 * j + 448] = gbuf[i]
    m = mid8[...]
    sq = jnp.sum(m * m, axis=1, keepdims=True)
    sq = sq + pltpu.roll(sq, 2, 0)
    sq = sq + pltpu.roll(sq, 4, 0)
    norm = (m * lax.rsqrt(sq * (1.0 / 7168.0) + EPS) * gain8[...]).astype(BF)
    xs[...] = norm
    for s in FAR:
        remote(
            xs, xbuf.at[chip], snd.at[6], rcv.at[6], (z, chip_at(s) * 2 + core)
        ).start()
    xbuf[chip] = norm
    sent(6, xbuf.at[pl.ds(0, 15)])
    r8w = iota((8, 1792), 0)
    for q in range(4):
        rows = m if q == 0 else pltpu.roll(m, 8 - 2 * q, 0)
        rows = jnp.where(r8w < 2, rows, 0.0)
        wd[128:144, 1792 * q : 1792 * (q + 1)] = jnp.concatenate(
            [rows, jnp.zeros_like(rows)], axis=0
        ).astype(BF)

    wait("wg", "wu", "wd", "wg2", "wu2", "wd2")
    drain(xbuf.at[pl.ds(0, 15)], rcv.at[6])
    x = xbuf[...].astype(F32).reshape(128, 1792).astype(BF)
    row_q = lax.rem(iota((128, 256), 0), 8) // 2
    both = jnp.zeros((128, 256), F32)
    for q in range(4):
        part = dot_t(x, gu[:, 1792 * q : 1792 * (q + 1)])
        both = both + jnp.where(row_q == q, part, 0.0)
    both = both + pltpu.roll(both, 126, 0)
    both = both + pltpu.roll(both, 124, 0)
    gate, up = both[:, :128], both[:, 128:]
    hidden = gate / (1.0 + jnp.exp(-gate)) * up * coefs
    keep = lax.rem(iota((128, 128), 0), 8) < 2
    hidden = jnp.where(keep, hidden, 0.0).astype(BF)
    r32, c128 = iota((32, 128), 0), iota((32, 128), 1)
    squeeze = jnp.where(c128 == 8 * (r32 // 2) + lax.rem(r32, 2), 1.0, 0.0).astype(BF)
    short = dot(squeeze, hidden).astype(BF)
    r32s, c16s = iota((32, 16), 0), iota((32, 16), 1)
    mine = (r32s // 2 == chip) & (chip == z) & (c16s == lax.rem(r32s, 2))
    short = jnp.concatenate([short, jnp.where(mine, 1.0, 0.0).astype(BF)], axis=1)
    for dx in (2, 1, 3, 0):
        q = lax.rem(chip // 4 + dx, 4)
        o = dot(short, wd[:, pl.ds(pl.multiple_of(1792 * q, 128), 1792)])
        for d in range(8):
            isend[8 * q + d] = o[:, 224 * d : 224 * d + 224].astype(BF)
        for dy in (2, 1, 3, 0):
            for k in range(2):
                if dx == 0 and dy == 0:
                    continue
                dst = chip_at(4 * dx + dy) * 2 + k
                remote(
                    isend.at[dst], ibuf.at[c], snd.at[7], rcv.at[7], (z, dst)
                ).start()
    remote(isend.at[sib], ibuf.at[c], snd.at[7], rcv.at[7], (z, sib)).start()
    ibuf[c] = isend[c]
    sent(7, ibuf.at[pl.ds(0, 31)])

    drain(ibuf.at[pl.ds(0, 31)], rcv.at[7])
    for k in range(2):
        acc = ibuf[k].astype(F32)
        for i in range(1, 16):
            acc = acc + ibuf[2 * i + k].astype(F32)
        for p in range(NZ):
            js[p, 2 * k : 2 * k + 2, :] = acc[2 * p : 2 * p + 2]
    for s in ZFAR:
        dst = lax.rem(z + s, NZ)
        remote(js.at[dst], jbuf.at[z], snd.at[8], rcv.at[8], (dst, c)).start()
    jbuf[z] = js[z]
    drain(jbuf.at[pl.ds(0, 15)], rcv.at[8])
    out_ref[...] = jnp.sum(jbuf[...], axis=0).astype(BF)

    sent(8, jbuf.at[pl.ds(0, 15)])
    wait(*list(todo))


def local(
    residual, query, latent_cache, lengths, w_uv, w_o, norm_gain, routes, route_weight,
    w_gate, w_up, w_down,
):
    hbm = pl.BlockSpec(memory_space=pltpu.HBM)
    vmem = pl.BlockSpec(memory_space=pltpu.VMEM)
    smem = pl.BlockSpec(memory_space=pltpu.SMEM)
    V = pltpu.VMEM
    D = pltpu.SemaphoreType.DMA
    return pl.pallas_call(
        body,
        out_shape=jax.ShapeDtypeStruct((4, 224), BF),
        in_specs=[smem] + [hbm] * 11,
        out_specs=vmem,
        scratch_shapes=[
            V((4, 4, 576), BF),
            V((2, 576, 1024), BF),
            V((4, 512, 128), BF),
            V((448, 512), BF),
            V((2, 448), BF),
            V((56, 128), BF),
            V((4, 64), jnp.int32),
            V((4, 64), F32),
            V((8, 1792), F32),
            V((256, 7168), BF),
            V((144, 7168), BF),
            V((2, 8, 576), BF),
            V((16, 2, 8, 576), BF),
            V((2, 16, 8, 640), BF),
            V((2, 16, 8, 640), BF),
            V((8, 256), BF),
            V((16, 8, 256), BF),
            V((16, 2, 2, 448), F32),
            V((32, 2, 448), F32),
            V((2, 448), F32),
            V((16, 2, 448), F32),
            V((8, 1792), F32),
            V((8, 1792), BF),
            V((16, 8, 1792), BF),
            V((32, 32, 224), BF),
            V((32, 32, 224), BF),
            V((16, 4, 224), F32),
            V((16, 4, 224), F32),
            D((11,)),
            D((4,)),
            D((4,)),
            D((9,)),
            D((9,)),
        ],
        compiler_params=pltpu.CompilerParams(
            collective_id=0, has_side_effects=True, vmem_limit_bytes=63 << 20
        ),
        name="decode_layer",
    )(
        lengths, query, jnp.swapaxes(latent_cache, 1, 2), w_uv, w_o.T, residual,
        norm_gain.reshape(56, 128), routes.T, route_weight.T,
        w_gate, w_up, w_down,
    )


def solution(mesh):
    in_specs = (
        P("ctx", "req"),
        P("req", "ctx", None),
        P("req", "ctx", None),
        P("req"),
        P("ctx", None, None),
        P("ctx", "req"),
        P(),
        P(),
        P(),
        P("req", "ctx", None),
        P("req", "ctx", None),
        P("req", "ctx", None),
    )
    return jax.shard_map(
        local, mesh=mesh, in_specs=in_specs, out_specs=P("req", "ctx"), check_vma=False
    )
```

```python
import jax
import jax.numpy as jnp
from jax import lax
from jax.experimental import pallas as pl
from jax.experimental.pallas import tpu as pltpu
from jax.sharding import PartitionSpec as P

MESH = pl.DeviceIdType.MESH
SCALE = 192.0 ** (-0.5)
NEG = -1e30
EPS = 1e-06
BF = jnp.bfloat16
F32 = jnp.float32
NZ = 16
NC = 32
NCHIP = 16
FAR = (10, 2, 8, 9, 11, 6, 14, 1, 3, 4, 12, 5, 7, 13, 15)
ZORD = (0, 1, 15, 2, 14, 3, 13, 4, 12, 5, 11, 6, 10, 7, 9, 8)
ZFAR = (8, 7, 9, 6, 10, 5, 11, 4, 12, 3, 13, 2, 14, 1, 15)


def dot(a, b):
    return jnp.dot(a, b, preferred_element_type=F32)


def dot_t(a, b):
    return lax.dot_general(a, b, (((1,), (1,)), ((), ())), preferred_element_type=F32)


def iota(shape, axis):
    return lax.broadcasted_iota(jnp.int32, shape, axis)


def body(
    lens_hbm, q_hbm, cache_hbm, wuv_hbm, wo_hbm, res_hbm, gain_hbm, routes_hbm, rw_hbm,
    wg_hbm, wu_hbm, wd_hbm,
    out_ref,
    lens, qin, cbuf, wuv, wo, res, gain, routes, rw, gain8, gu, wd, wdp,
    qs, qbuf, osend, obuf, vs, vbuf, fs, fbuf, gs, gbuf, mid8, mids, midbuf, xs, xbuf,
    hs, hb, isend, ibuf, js, jbuf,
    loc, sib_s, sib_r, snd, rcv,
):
    z = lax.axis_index("req")
    c = lax.axis_index("ctx")
    core = lax.rem(c, 2)
    chip = c // 2
    sib = c + 1 - 2 * core

    def chip_at(s):
        x = lax.rem(chip // 4 + s // 4, 4)
        y = lax.rem(lax.rem(chip, 4) + s % 4, 4)
        return x * 4 + y

    def back(s):
        return ((4 - s // 4) % 4) * 4 + (4 - s % 4) % 4

    todo = {}

    def begin(name, copy):
        copy.start()
        todo[name] = copy.wait

    def wait(*names):
        for name in names:
            todo.pop(name)()

    def drain(ref, sem):
        pltpu.make_async_copy(ref, ref, sem).wait()

    own, other = pl.ds(0, 512), pl.ds(512, 512)
    first = pl.ds(pl.multiple_of(64 * core, 64), 64)
    second = pl.ds(pl.multiple_of(128 + 64 * core, 64), 64)
    for i, (name, src, dst) in enumerate((
        ("q", q_hbm, qin),
        ("cache", cache_hbm, cbuf.at[:, :, own]),
        ("gain", gain_hbm, gain),
        ("routes", routes_hbm, routes),
        ("rw", rw_hbm, rw),
        ("res", res_hbm, res),
        ("wuv", wuv_hbm, wuv),
        ("wo", wo_hbm, wo),
        ("wg", wg_hbm.at[0], gu.at[first]),
        ("wu", wu_hbm.at[0], gu.at[second]),
        ("wd", wd_hbm.at[0], wd.at[first]),
        ("lens", lens_hbm, lens),
    )):
        begin(name, pltpu.make_async_copy(src, dst, loc.at[i]))

    barrier = pltpu.get_barrier_semaphore()

    for s in ZFAR:
        pl.semaphore_signal(
            barrier, inc=1, device_id=(lax.rem(z + s, NZ), c), device_id_type=MESH
        )

    @pl.loop(1, NC)
    def _(s):
        pl.semaphore_signal(
            barrier, inc=1, device_id=(z, lax.rem(c + s, NC)), device_id_type=MESH
        )

    pl.semaphore_wait(barrier, NC + NZ - 2)

    def remote(src, dst, send, recv, dev):
        return pltpu.make_async_remote_copy(
            src_ref=src, dst_ref=dst, send_sem=send, recv_sem=recv,
            device_id=dev, device_id_type=MESH,
        )

    def twin(i, name, src, dst):
        copy = remote(src, dst, sib_s.at[i], sib_r.at[i], (z, sib))
        copy.start()
        todo[name] = copy.wait_recv
        todo[name + "_sent"] = copy.wait_send

    def sent(i, ref):
        todo["sent%d" % i] = lambda: drain(ref, snd.at[i])

    wait("q")
    for r in range(2):
        rows = jnp.concatenate(
            [qin[2 * r].astype(F32), qin[2 * r + 1].astype(F32)], axis=0
        ).astype(BF)
        qs[r] = rows
        qbuf[0, r] = rows
    twin(0, "cache2", cache_hbm, cbuf.at[:, :, other])
    for s in FAR:
        remote(
            qs, qbuf.at[back(s)], snd.at[0], rcv.at[0], (z, chip_at(s) * 2 + core)
        ).start()
    sent(0, qbuf.at[pl.ds(0, 15)])
    twin(1, "wg2", wg_hbm.at[0], gu.at[first])
    twin(2, "wu2", wu_hbm.at[0], gu.at[second])
    twin(3, "wd2", wd_hbm.at[0], wd.at[first])

    wait("gain", "routes", "rw")
    g = gain[...].astype(F32)
    for i in range(56):
        q, j = i // 14, i % 14
        gain8[2 * q : 2 * q + 2, 128 * j : 128 * j + 128] = jnp.broadcast_to(
            g[i : i + 1], (2, 128)
        )
    match = jnp.where(routes[...] == z, 1.0, 0.0)
    coef = jnp.sum(match * rw[...], axis=0, keepdims=True)
    row = iota((128, 64), 0)
    token = 4 * (row // 8) + 2 * core + lax.rem(row, 2)
    pick = (token == iota((128, 64), 1)) & (lax.rem(row, 8) < 2)
    coefs = jnp.sum(jnp.where(pick, coef, 0.0), axis=1, keepdims=True)
    match8 = jnp.broadcast_to(jnp.sum(match, axis=0, keepdims=True), (8, 64)).astype(BF)
    i64, j64 = iota((64, 64), 0), iota((64, 64), 1)
    rank8 = dot(match8, jnp.where(i64 < j64, 1.0, 0.0).astype(BF)).astype(BF)
    pick = jnp.where(pick, 1.0, 0.0).astype(BF)
    fill = (dot_t(match8, pick)[:1] > 0.5) & (
        dot_t(rank8, pick)[:1] == iota((32, 128), 0).astype(F32)
    )
    fill = jnp.where(fill, 1.0, 0.0).astype(BF)
    named = dot_t(jnp.where(i64 == j64, 1.0, 0.0).astype(BF), match8)[:, :1]
    ranks = dot_t(jnp.where(j64 < i64, 1.0, 0.0).astype(BF), match8)[:, :1]
    spread = (named > 0.5) & (ranks == iota((64, 32), 1).astype(F32))
    spread = jnp.where(spread, 1.0, 0.0).astype(BF)

    wait("cache", "cache2", "lens")
    drain(qbuf.at[pl.ds(1, 15)], rcv.at[0])
    row_k = lax.rem(iota((128, 1024), 0) // 4, 2)
    lane_p = iota((128, 1024), 1)
    place = jnp.where(lane_p < 512, c * 512 + lane_p, sib * 512 + lane_p - 512)
    lane_e = iota((128, 128), 1)
    for r in range(2):
        ql = qbuf[:, r].astype(F32).reshape(128, 576).astype(BF)
        see = place <= lens[r] - 2 + row_k
        score = jnp.where(see, dot(ql, cbuf[r]) * SCALE, NEG)
        peak = jnp.max(score, axis=1, keepdims=True)
        peak = jnp.where(peak > 0.5 * NEG, peak, 0.0)
        raised = jnp.exp(score - peak)
        total = jnp.sum(raised, axis=1, keepdims=True)
        mixed = dot_t(raised.astype(BF), cbuf[r, :512])
        filled = total > 0.0
        safe = jnp.where(filled, total, 1.0)
        part = jnp.where(filled, mixed / safe, 0.0)
        log = jnp.where(filled, peak + jnp.log(safe), NEG)
        hi = log.astype(BF).astype(F32)
        mi = (log - hi).astype(BF).astype(F32)
        lo = log - hi - mi
        tail = jnp.where(
            lane_e == 0, hi, jnp.where(lane_e == 1, mi, jnp.where(lane_e == 2, lo, 0.0))
        )
        osend[r, :, :, :512] = part.reshape(16, 8, 512).astype(BF)
        osend[r, :, :, 512:] = tail.reshape(16, 8, 128).astype(BF)
        for s in FAR:
            remote(
                osend.at[r, s], obuf.at[r, back(s)], snd.at[1 + r], rcv.at[1 + r],
                (z, chip_at(s) * 2 + core),
            ).start()
        obuf[r, 0] = osend[r, 0]
        sent(1 + r, obuf.at[r, pl.ds(0, 15)])

    wait("wuv")
    latents = []
    for r in range(2):
        drain(obuf.at[r, pl.ds(1, 15)], rcv.at[1 + r])
        logs = jnp.sum(obuf[r, :, :, 512:].astype(F32), axis=2, keepdims=True)
        top = jnp.max(logs, axis=0, keepdims=True)
        factor = jnp.exp(logs - top)
        numer = jnp.sum(factor * obuf[r, :, :, :512].astype(F32), axis=0)
        latents.append(numer / jnp.sum(factor, axis=0))
    latent = jnp.concatenate(latents, axis=0).astype(BF)
    r8, c16 = iota((8, 16), 0), iota((8, 16), 1)
    halves = [None, None]
    for h in range(4):
        pick = (r8 // 4 == h // 2) & (c16 == 4 * lax.rem(r8, 4) + h)
        rows = dot(jnp.where(pick, 1.0, 0.0).astype(BF), latent).astype(BF)
        val = dot(rows, wuv[h])
        halves[h % 2] = val if halves[h % 2] is None else halves[h % 2] + val
    vrow = jnp.concatenate(halves, axis=1).astype(BF)
    vs[...] = vrow
    vbuf[0] = vrow
    for s in ZFAR:
        pos = ZORD.index(NZ - s)
        remote(
            vs, vbuf.at[pos], snd.at[3], rcv.at[3 if pos < 12 else 9],
            (lax.rem(z + s, NZ), c),
        ).start()
    sent(3, vbuf.at[pl.ds(0, 15)])

    wait("wo")
    for lo, n in ((0, 12), (12, 4)):
        if lo == 0:
            drain(vbuf.at[pl.ds(1, 11)], rcv.at[3])
        else:
            drain(vbuf.at[pl.ds(12, 4)], rcv.at[9])
        vals = vbuf[lo : lo + n].astype(F32).reshape(8 * n, 256).astype(BF)
        y0 = dot_t(vals, wo[:, :256])
        y1 = dot_t(vals, wo[:, 256:])
        y = (y0 + pltpu.roll(y1, 8 * n - 4, 0)).reshape(n, 8, 448)
        fs[lo : lo + n, 0] = y[:, 0:2]
        fs[lo : lo + n, 1] = y[:, 2:4]
        for pos in range(lo, lo + n):
            for k in range(2):
                dst = 2 * lax.rem(z + ZORD[pos], NZ) + k

                @pl.when(dst != c)
                def _():
                    remote(
                        fs.at[pos, k], fbuf.at[c], snd.at[4], rcv.at[4], (z, dst)
                    ).start()

                @pl.when(dst == c)
                def _():
                    fbuf[c] = fs[pos, k]
    sent(4, fbuf.at[pl.ds(0, 31)])

    wait("res")
    drain(fbuf.at[pl.ds(0, 31)], rcv.at[4])
    mid = (jnp.sum(fbuf[...], axis=0) + res[...].astype(F32)).astype(BF)
    gs[...] = mid
    for s in ZFAR:
        remote(
            gs, gbuf.at[z], snd.at[5], rcv.at[5], (lax.rem(z + s, NZ), c)
        ).start()
    gbuf[z] = mid
    sent(5, gbuf.at[pl.ds(0, 15)])

    wait("wd", "wd2")
    for k in range(2):
        @pl.when(core == k)
        def _():
            for i in range(NCHIP):
                at = 448 * i + 224 * k
                wdp[i, :, :224] = wd[:, at : at + 224]

    drain(gbuf.at[pl.ds(0, 15)], rcv.at[5])
    for i in range(NZ):
        q, j = i // 4, i % 4
        mid8[2 * q : 2 * q + 2, 448 * j : 448 * j + 448] = gbuf[i].astype(F32)
    m = mid8[...]
    sq = jnp.sum(m * m, axis=1, keepdims=True)
    sq = sq + pltpu.roll(sq, 2, 0)
    sq = sq + pltpu.roll(sq, 4, 0)
    norm = (m * lax.rsqrt(sq * (1.0 / 7168.0) + EPS) * gain8[...]).astype(BF)
    xs[...] = norm
    for s in FAR:
        remote(
            xs, xbuf.at[chip], snd.at[6], rcv.at[6], (z, chip_at(s) * 2 + core)
        ).start()
    xbuf[chip] = norm
    sent(6, xbuf.at[pl.ds(0, 15)])

    @pl.when(chip == z)
    def _():
        for d in range(NC):
            q, j = d // 8, d % 8
            mids[d] = mid8[2 * q : 2 * q + 2, 224 * j : 224 * j + 224]

        @pl.loop(1, NC)
        def _(s):
            dst = lax.rem(c + s, NC)
            remote(
                mids.at[dst], midbuf.at[core], snd.at[9], rcv.at[10], (z, dst)
            ).start()

        midbuf[core] = mids[c]

    wait("wg", "wu", "wg2", "wu2")
    drain(xbuf.at[pl.ds(0, 15)], rcv.at[6])
    x = xbuf[...].astype(F32).reshape(128, 1792).astype(BF)
    row_q = lax.rem(iota((128, 256), 0), 8) // 2
    both = jnp.zeros((128, 256), F32)
    for q in range(4):
        part = dot_t(x, gu[:, 1792 * q : 1792 * (q + 1)])
        both = both + jnp.where(row_q == q, part, 0.0)
    both = both + pltpu.roll(both, 126, 0)
    both = both + pltpu.roll(both, 124, 0)
    gate, up = both[:, :128], both[:, 128:]
    hidden = gate / (1.0 + jnp.exp(-gate)) * up * coefs
    keep = lax.rem(iota((128, 128), 0), 8) < 2
    hidden = jnp.where(keep, hidden, 0.0).astype(BF)
    short = dot(fill, hidden)
    hs[...] = short.astype(BF)
    twin(4, "hidden", hs, hb)
    wait("hidden")
    short = (short + hb[...].astype(F32)).astype(BF)
    order = FAR + (0,)
    for lo in range(0, NCHIP, 4):
        for s in order[lo : lo + 4]:
            isend[s] = dot(short, wdp[chip_at(s)])[:, :224].astype(BF)
        for s in order[lo : lo + 4]:
            if s:
                remote(
                    isend.at[s], ibuf.at[back(s)], snd.at[7], rcv.at[7],
                    (z, chip_at(s) * 2 + core),
                ).start()
    ibuf[0] = isend[0]
    sent(7, ibuf.at[pl.ds(0, 15)])

    drain(ibuf.at[pl.ds(1, 15)], rcv.at[7])
    acc = jnp.sum(ibuf[...].astype(F32), axis=0)
    hi = acc.astype(BF)
    mi = (acc - hi.astype(F32)).astype(BF)
    lo = (acc - hi.astype(F32) - mi.astype(F32)).astype(BF)
    acc = dot(spread, hi) + dot(spread, mi) + dot(spread, lo)
    for p in range(NZ):
        js[p] = acc[4 * p : 4 * p + 4]
    for s in ZFAR:
        dst = lax.rem(z + s, NZ)
        remote(js.at[dst], jbuf.at[z], snd.at[8], rcv.at[8], (dst, c)).start()
    jbuf[z] = js[z]
    drain(jbuf.at[pl.ds(0, 15)], rcv.at[8])
    last = jnp.sum(jbuf[...], axis=0)

    @pl.when(chip == z)
    def _():
        drain(midbuf.at[0], rcv.at[10])
        drain(mids.at[pl.ds(0, 31)], snd.at[9])

    @pl.when(chip != z)
    def _():
        drain(midbuf, rcv.at[10])

    mid = jnp.concatenate([midbuf[0], midbuf[1]], axis=0)
    out_ref[...] = (last + mid).astype(BF)
    sent(8, jbuf.at[pl.ds(0, 15)])
    wait(*list(todo))


def local(
    residual, query, latent_cache, lengths, w_uv, w_o, norm_gain, routes, route_weight,
    w_gate, w_up, w_down,
):
    hbm = pl.BlockSpec(memory_space=pltpu.HBM)
    vmem = pl.BlockSpec(memory_space=pltpu.VMEM)
    V = pltpu.VMEM
    D = pltpu.SemaphoreType.DMA
    return pl.pallas_call(
        body,
        out_shape=jax.ShapeDtypeStruct((4, 224), BF),
        in_specs=[hbm] * 12,
        out_specs=vmem,
        scratch_shapes=[
            pltpu.SMEM((2,), jnp.int32),
            V((4, 4, 576), BF),
            V((2, 576, 1024), BF),
            V((4, 512, 128), BF),
            V((448, 512), BF),
            V((2, 448), BF),
            V((56, 128), BF),
            V((4, 64), jnp.int32),
            V((4, 64), F32),
            V((8, 1792), F32),
            V((256, 7168), BF),
            V((128, 7168), BF),
            V((16, 128, 256), BF),
            V((2, 8, 576), BF),
            V((16, 2, 8, 576), BF),
            V((2, 16, 8, 640), BF),
            V((2, 16, 8, 640), BF),
            V((8, 256), BF),
            V((16, 8, 256), BF),
            V((16, 2, 2, 448), F32),
            V((32, 2, 448), F32),
            V((2, 448), BF),
            V((16, 2, 448), BF),
            V((8, 1792), F32),
            V((32, 2, 224), F32),
            V((2, 2, 224), F32),
            V((8, 1792), BF),
            V((16, 8, 1792), BF),
            V((32, 128), BF),
            V((32, 128), BF),
            V((16, 32, 224), BF),
            V((16, 32, 224), BF),
            V((16, 4, 224), F32),
            V((16, 4, 224), F32),
            D((12,)),
            D((5,)),
            D((5,)),
            D((10,)),
            D((11,)),
        ],
        compiler_params=pltpu.CompilerParams(
            collective_id=0, has_side_effects=True, vmem_limit_bytes=48 << 20
        ),
        name="decode_layer",
    )(
        *[
            pltpu.with_memory_space_constraint(x, pltpu.HBM)
            for x in (
                lengths, query, jnp.swapaxes(latent_cache, 1, 2), w_uv, w_o.T, residual,
                norm_gain.reshape(56, 128), routes.T, route_weight.T,
                w_gate, w_up, w_down,
            )
        ],
    )


def solution(mesh):
    in_specs = (
        P("ctx", "req"),
        P("req", "ctx", None),
        P("req", "ctx", None),
        P("req"),
        P("ctx", None, None),
        P("ctx", "req"),
        P(),
        P(),
        P(),
        P("req", "ctx", None),
        P("req", "ctx", None),
        P("req", "ctx", None),
    )
    return jax.shard_map(
        local, mesh=mesh, in_specs=in_specs, out_specs=P("req", "ctx"), check_vma=False
    )
```

```python
import jax
import jax.numpy as jnp
from jax import lax
from jax.experimental import pallas as pl
from jax.experimental.pallas import tpu as pltpu
from jax.sharding import PartitionSpec as P

MESH = pl.DeviceIdType.MESH
SCALE = 192.0 ** (-0.5)
NEG = -1e30
EPS = 1e-06
BF = jnp.bfloat16
F32 = jnp.float32
NZ = 16
NC = 32
NCHIP = 16
FAR = (10, 2, 8, 9, 11, 6, 14, 1, 3, 4, 12, 5, 7, 13, 15)
ZORD = (0, 1, 15, 2, 14, 3, 13, 4, 12, 5, 11, 6, 10, 7, 9, 8)
PAIRS = ((0, 1, 7, 2), (6, 3, 5, 4))
ZFAR = (8, 7, 9, 6, 10, 5, 11, 4, 12, 3, 13, 2, 14, 1, 15)


def dot(a, b):
    return jnp.dot(a, b, preferred_element_type=F32)


def dot_t(a, b):
    return lax.dot_general(a, b, (((1,), (1,)), ((), ())), preferred_element_type=F32)


def iota(shape, axis):
    return lax.broadcasted_iota(jnp.int32, shape, axis)


def body(
    lens_hbm, q_hbm, cache_hbm, wuv_hbm, wo_hbm, res_hbm, gain_hbm, routes_hbm, rw_hbm,
    wg_hbm, wu_hbm, wd_hbm,
    out_ref,
    lens, qin, cbuf, wuv, wo, res, gain, routes, rw, table, gain8, gu, wd, wdp,
    qs, qbuf, osend, obuf, vs, vbuf, fs, fbuf, gs, gbuf, mid8, mids, midbuf, xs, xs2, xbuf, xbuf2,
    hs, hb, isend, ibuf, js, jbuf,
    loc, sib_s, sib_r, snd, rcv,
):
    z = lax.axis_index("req")
    c = lax.axis_index("ctx")
    core = lax.rem(c, 2)
    chip = c // 2
    sib = c + 1 - 2 * core

    def chip_at(s):
        x = lax.rem(chip // 4 + s // 4, 4)
        y = lax.rem(lax.rem(chip, 4) + s % 4, 4)
        return x * 4 + y

    def back(s):
        return ((4 - s // 4) % 4) * 4 + (4 - s % 4) % 4

    todo = {}

    def begin(name, copy):
        copy.start()
        todo[name] = copy.wait

    def wait(*names):
        for name in names:
            todo.pop(name)()

    def drain(ref, sem):
        pltpu.make_async_copy(ref, ref, sem).wait()

    own, other = pl.ds(0, 512), pl.ds(512, 512)
    first = pl.ds(pl.multiple_of(64 * core, 64), 64)
    second = pl.ds(pl.multiple_of(128 + 64 * core, 64), 64)
    for i, (name, src, dst) in enumerate((
        ("q", q_hbm, qin),
        ("cache0", cache_hbm.at[0], cbuf.at[0, :, own]),
        ("cache1", cache_hbm.at[1], cbuf.at[1, :, own]),
        ("gain", gain_hbm, gain),
        ("routes", routes_hbm, routes),
        ("rw", rw_hbm, rw),
        ("res", res_hbm, res),
        ("wuv", wuv_hbm, wuv),
        ("wo", wo_hbm, wo),
        ("wg", wg_hbm.at[0], gu.at[first]),
        ("wu", wu_hbm.at[0], gu.at[second]),
        ("wd", wd_hbm.at[0], wd.at[first]),
        ("lens", lens_hbm, lens),
    )):
        begin(name, pltpu.make_async_copy(src, dst, loc.at[i]))

    barrier = pltpu.get_barrier_semaphore()

    for s in ZFAR:
        pl.semaphore_signal(
            barrier, inc=1, device_id=(lax.rem(z + s, NZ), c), device_id_type=MESH
        )

    @pl.loop(1, NC)
    def _(s):
        pl.semaphore_signal(
            barrier, inc=1, device_id=(z, lax.rem(c + s, NC)), device_id_type=MESH
        )

    pl.semaphore_wait(barrier, NC + NZ - 2)

    def remote(src, dst, send, recv, dev):
        return pltpu.make_async_remote_copy(
            src_ref=src, dst_ref=dst, send_sem=send, recv_sem=recv,
            device_id=dev, device_id_type=MESH,
        )

    def twin(i, name, src, dst):
        copy = remote(src, dst, sib_s.at[i], sib_r.at[i], (z, sib))
        copy.start()
        todo[name] = copy.wait_recv
        todo[name + "_sent"] = copy.wait_send

    def sent(i, ref):
        todo["sent%d" % i] = lambda: drain(ref, snd.at[i])

    wait("q")
    for r in range(2):
        rows = jnp.concatenate(
            [qin[2 * r].astype(F32), qin[2 * r + 1].astype(F32)], axis=0
        ).astype(BF)
        qs[r] = rows
        qbuf[r, 0] = rows
    for r in range(2):
        twin(5 + r, "twin%d" % r, cache_hbm.at[r], cbuf.at[r, :, other])
    for r in range(2):
        for s in FAR:
            remote(
                qs.at[r], qbuf.at[r, back(s)], snd.at[0], rcv.at[0 if r == 0 else 11],
                (z, chip_at(s) * 2 + core),
            ).start()
    sent(0, qbuf.at[:, pl.ds(0, 15)])
    twin(1, "wg2", wg_hbm.at[0], gu.at[first])
    twin(2, "wu2", wu_hbm.at[0], gu.at[second])
    twin(3, "wd2", wd_hbm.at[0], wd.at[first])

    wait("gain", "routes", "rw")
    g = gain[...].astype(F32)
    for i in range(56):
        m, j = i // 7, i % 7
        table[m, :, 128 * j : 128 * j + 128] = jnp.broadcast_to(g[i : i + 1], (2, 128))

    def pair(far, j):
        return lax.rem(z // 2 + PAIRS[far][j], 8)

    for far in range(2):
        for j in range(4):
            gain8[far, 2 * j : 2 * j + 2] = table[pair(far, j)]
    match = jnp.where(routes[...] == z, 1.0, 0.0)
    coef = jnp.sum(match * rw[...], axis=0, keepdims=True)
    row = iota((128, 64), 0)
    token = 4 * (row // 8) + 2 * core + lax.rem(row, 2)
    pick = (token == iota((128, 64), 1)) & (lax.rem(row, 8) < 2)
    coefs = jnp.sum(jnp.where(pick, coef, 0.0), axis=1, keepdims=True)
    match8 = jnp.broadcast_to(jnp.sum(match, axis=0, keepdims=True), (8, 64)).astype(BF)
    i64, j64 = iota((64, 64), 0), iota((64, 64), 1)
    rank8 = dot(match8, jnp.where(i64 < j64, 1.0, 0.0).astype(BF)).astype(BF)
    pick = jnp.where(pick, 1.0, 0.0).astype(BF)
    fill = (dot_t(match8, pick)[:1] > 0.5) & (
        dot_t(rank8, pick)[:1] == iota((32, 128), 0).astype(F32)
    )
    fill = jnp.where(fill, 1.0, 0.0).astype(BF)
    named = dot_t(jnp.where(i64 == j64, 1.0, 0.0).astype(BF), match8)[:, :1]
    ranks = dot_t(jnp.where(j64 < i64, 1.0, 0.0).astype(BF), match8)[:, :1]
    spread = (named > 0.5) & (ranks == iota((64, 32), 1).astype(F32))
    spread = jnp.where(spread, 1.0, 0.0).astype(BF)

    wait("lens")
    row_k = lax.rem(iota((128, 1024), 0) // 4, 2)
    lane_p = iota((128, 1024), 1)
    place = jnp.where(lane_p < 512, c * 512 + lane_p, sib * 512 + lane_p - 512)
    lane_e = iota((128, 128), 1)
    for r in range(2):
        wait("cache%d" % r, "twin%d" % r)
        drain(qbuf.at[r, pl.ds(1, 15)], rcv.at[0 if r == 0 else 11])
        ql = qbuf[r].astype(F32).reshape(128, 576).astype(BF)
        see = place <= lens[r] - 2 + row_k
        score = jnp.where(see, dot(ql, cbuf[r]) * SCALE, NEG)
        peak = jnp.max(score, axis=1, keepdims=True)
        peak = jnp.where(peak > 0.5 * NEG, peak, 0.0)
        raised = jnp.exp(score - peak)
        total = jnp.sum(raised, axis=1, keepdims=True)
        mixed = dot_t(raised.astype(BF), cbuf[r, :512])
        filled = total > 0.0
        safe = jnp.where(filled, total, 1.0)
        part = jnp.where(filled, mixed / safe, 0.0)
        log = jnp.where(filled, peak + jnp.log(safe), NEG)
        hi = log.astype(BF).astype(F32)
        mi = (log - hi).astype(BF).astype(F32)
        lo = log - hi - mi
        tail = jnp.where(
            lane_e == 0, hi, jnp.where(lane_e == 1, mi, jnp.where(lane_e == 2, lo, 0.0))
        )
        osend[r, :, :, :512] = part.reshape(16, 8, 512).astype(BF)
        osend[r, :, :, 512:] = tail.reshape(16, 8, 128).astype(BF)
        for s in FAR:
            remote(
                osend.at[r, s], obuf.at[r, back(s)], snd.at[1 + r], rcv.at[1 + r],
                (z, chip_at(s) * 2 + core),
            ).start()
        obuf[r, 0] = osend[r, 0]
        sent(1 + r, obuf.at[r, pl.ds(0, 15)])

    wait("wuv")
    latents = []
    for r in range(2):
        drain(obuf.at[r, pl.ds(1, 15)], rcv.at[1 + r])
        logs = jnp.sum(obuf[r, :, :, 512:].astype(F32), axis=2, keepdims=True)
        top = jnp.max(logs, axis=0, keepdims=True)
        factor = jnp.exp(logs - top)
        numer = jnp.sum(factor * obuf[r, :, :, :512].astype(F32), axis=0)
        latents.append(numer / jnp.sum(factor, axis=0))
    latent = jnp.concatenate(latents, axis=0).astype(BF)
    r8, c16 = iota((8, 16), 0), iota((8, 16), 1)
    halves = [None, None]
    for h in range(4):
        pick = (r8 // 4 == h // 2) & (c16 == 4 * lax.rem(r8, 4) + h)
        rows = dot(jnp.where(pick, 1.0, 0.0).astype(BF), latent).astype(BF)
        val = dot(rows, wuv[h])
        halves[h % 2] = val if halves[h % 2] is None else halves[h % 2] + val
    vrow = jnp.concatenate(halves, axis=1).astype(BF)
    vs[...] = vrow
    vbuf[0] = vrow
    for s in ZFAR:
        pos = ZORD.index(NZ - s)
        remote(
            vs, vbuf.at[pos], snd.at[3], rcv.at[3 if pos < 12 else 9],
            (lax.rem(z + s, NZ), c),
        ).start()
    sent(3, vbuf.at[pl.ds(0, 15)])

    wait("wo")
    for lo, n in ((0, 12), (12, 4)):
        if lo == 0:
            drain(vbuf.at[pl.ds(1, 11)], rcv.at[3])
        else:
            drain(vbuf.at[pl.ds(12, 4)], rcv.at[9])
        vals = vbuf[lo : lo + n].astype(F32).reshape(8 * n, 256).astype(BF)
        y0 = dot_t(vals, wo[:, :256])
        y1 = dot_t(vals, wo[:, 256:])
        y = (y0 + pltpu.roll(y1, 8 * n - 4, 0)).reshape(n, 8, 448)
        fs[lo : lo + n, 0] = y[:, 0:2]
        fs[lo : lo + n, 1] = y[:, 2:4]
        for pos in range(lo, lo + n):
            for k in range(2):
                dst = 2 * lax.rem(z + ZORD[pos], NZ) + k

                @pl.when(dst != c)
                def _():
                    remote(
                        fs.at[pos, k], fbuf.at[c], snd.at[4], rcv.at[4], (z, dst)
                    ).start()

                @pl.when(dst == c)
                def _():
                    fbuf[c] = fs[pos, k]
    sent(4, fbuf.at[pl.ds(0, 31)])

    wait("res")
    drain(fbuf.at[pl.ds(0, 31)], rcv.at[4])
    mid = (jnp.sum(fbuf[...], axis=0) + res[...].astype(F32)).astype(BF)
    gs[...] = mid
    for s in ZFAR:
        near = [(0 - (s + k) // 2) % 8 in PAIRS[0] for k in range(2)]
        sem = 5 if all(near) else 12
        if any(near) and not all(near):
            even = lax.rem(z, 2) == 0
            sem = jnp.where(even, 5 if near[0] else 12, 5 if near[1] else 12)
        remote(
            gs, gbuf.at[z], snd.at[5], rcv.at[sem], (lax.rem(z + s, NZ), c)
        ).start()
    gbuf[z] = mid
    sent(5, gbuf.at[pl.ds(0, 15)])

    wait("wd", "wd2")
    for k in range(2):
        @pl.when(core == k)
        def _():
            for i in range(NCHIP):
                at = 448 * i + 224 * k
                wdp[i, :, :224] = wd[:, at : at + 224]

    lane_w = iota((8, 128), 1)
    sq = jnp.zeros((8, 1), F32)
    for far in range(2):
        if far == 0:
            drain(gbuf.at[pl.ds(0, 7)], rcv.at[5])
        else:
            drain(gbuf.at[pl.ds(0, 8)], rcv.at[12])
        for j in range(4):
            for b in range(2):
                mid8[far, 2 * j : 2 * j + 2, 448 * b : 448 * b + 448] = gbuf[
                    2 * pair(far, j) + b
                ].astype(F32)
        m = mid8[far]
        sq = sq + jnp.sum(m * m, axis=1, keepdims=True)
        gained = (m * gain8[far]).astype(BF)
        if far == 0:
            src, dst, i = xs, xbuf, 6
        else:
            sq = sq + pltpu.roll(sq, 2, 0)
            sq = sq + pltpu.roll(sq, 4, 0)
            norm = lax.rsqrt(sq * (1.0 / 7168.0) + EPS)
            src, dst, i = xs2, xbuf2, 10
            hi = norm.astype(BF).astype(F32)
            mi = (norm - hi).astype(BF).astype(F32)
            tail = jnp.where(
                lane_w == 0,
                hi,
                jnp.where(lane_w == 1, mi, jnp.where(lane_w == 2, norm - hi - mi, 0.0)),
            ).astype(BF)
            gained = jnp.concatenate([gained, tail], axis=1)
        src[...] = gained
        for s in FAR:
            remote(
                src, dst.at[chip], snd.at[i], rcv.at[6 if far == 0 else 13],
                (z, chip_at(s) * 2 + core),
            ).start()
        dst[chip] = gained
        sent(i, dst.at[pl.ds(0, 15)])

    @pl.when(chip == z)
    def _():
        for far in range(2):
            for j in range(4):
                for d in range(4):
                    mids[4 * pair(far, j) + d] = mid8[
                        far, 2 * j : 2 * j + 2, 224 * d : 224 * d + 224
                    ]

        @pl.loop(1, NC)
        def _(s):
            dst = lax.rem(c + s, NC)
            remote(
                mids.at[dst], midbuf.at[core], snd.at[9], rcv.at[10], (z, dst)
            ).start()

        midbuf[core] = mids[c]

    wait("wg", "wu", "wg2", "wu2")
    row_j = lax.rem(iota((128, 256), 0), 8) // 2
    both = jnp.zeros((128, 256), F32)
    for far in range(2):
        if far == 0:
            drain(xbuf.at[pl.ds(0, 15)], rcv.at[6])
            x = xbuf[...].astype(F32)
        else:
            drain(xbuf2.at[pl.ds(0, 15)], rcv.at[13])
            x = xbuf2[...].astype(F32)
        x = x.reshape(128, 896 + 128 * far)
        if far:
            norm = jnp.sum(x[:, 896:], axis=1, keepdims=True)
        x = x[:, :896].astype(BF)
        for j in range(4):
            at = pl.multiple_of(896 * pair(far, j), 128)
            part = dot_t(x, gu[:, pl.ds(at, 896)])
            both = both + jnp.where(row_j == j, part, 0.0)
    both = both + pltpu.roll(both, 126, 0)
    both = (both + pltpu.roll(both, 124, 0)) * norm
    gate, up = both[:, :128], both[:, 128:]
    hidden = gate / (1.0 + jnp.exp(-gate)) * up * coefs
    keep = lax.rem(iota((128, 128), 0), 8) < 2
    hidden = jnp.where(keep, hidden, 0.0).astype(BF)
    short = dot(fill, hidden)
    hs[...] = short.astype(BF)
    twin(4, "hidden", hs, hb)
    wait("hidden")
    short = (short + hb[...].astype(F32)).astype(BF)
    order = FAR + (0,)
    for lo in range(0, NCHIP, 4):
        for s in order[lo : lo + 4]:
            isend[s] = dot(short, wdp[chip_at(s)])[:, :224].astype(BF)
        for s in order[lo : lo + 4]:
            if s:
                remote(
                    isend.at[s], ibuf.at[back(s)], snd.at[7], rcv.at[7],
                    (z, chip_at(s) * 2 + core),
                ).start()
    ibuf[0] = isend[0]
    sent(7, ibuf.at[pl.ds(0, 15)])

    drain(ibuf.at[pl.ds(1, 15)], rcv.at[7])
    acc = jnp.sum(ibuf[...].astype(F32), axis=0)
    hi = acc.astype(BF)
    mi = (acc - hi.astype(F32)).astype(BF)
    lo = (acc - hi.astype(F32) - mi.astype(F32)).astype(BF)
    acc = dot(spread, hi) + dot(spread, mi) + dot(spread, lo)
    for p in range(NZ):
        js[p] = acc[4 * p : 4 * p + 4]
    for s in ZFAR:
        dst = lax.rem(z + s, NZ)
        remote(js.at[dst], jbuf.at[z], snd.at[8], rcv.at[8], (dst, c)).start()
    jbuf[z] = js[z]
    drain(jbuf.at[pl.ds(0, 15)], rcv.at[8])
    last = jnp.sum(jbuf[...], axis=0)

    @pl.when(chip == z)
    def _():
        drain(midbuf.at[0], rcv.at[10])
        drain(mids.at[pl.ds(0, 31)], snd.at[9])

    @pl.when(chip != z)
    def _():
        drain(midbuf, rcv.at[10])

    mid = jnp.concatenate([midbuf[0], midbuf[1]], axis=0)
    out_ref[...] = (last + mid).astype(BF)
    sent(8, jbuf.at[pl.ds(0, 15)])
    wait(*list(todo))


def local(
    residual, query, latent_cache, lengths, w_uv, w_o, norm_gain, routes, route_weight,
    w_gate, w_up, w_down,
):
    hbm = pl.BlockSpec(memory_space=pltpu.HBM)
    vmem = pl.BlockSpec(memory_space=pltpu.VMEM)
    V = pltpu.VMEM
    D = pltpu.SemaphoreType.DMA
    return pl.pallas_call(
        body,
        out_shape=jax.ShapeDtypeStruct((4, 224), BF),
        in_specs=[hbm] * 12,
        out_specs=vmem,
        scratch_shapes=[
            pltpu.SMEM((2,), jnp.int32),
            V((4, 4, 576), BF),
            V((2, 576, 1024), BF),
            V((4, 512, 128), BF),
            V((448, 512), BF),
            V((2, 448), BF),
            V((56, 128), BF),
            V((4, 64), jnp.int32),
            V((4, 64), F32),
            V((8, 2, 896), F32),
            V((2, 8, 896), F32),
            V((256, 7168), BF),
            V((128, 7168), BF),
            V((16, 128, 256), BF),
            V((2, 8, 576), BF),
            V((2, 16, 8, 576), BF),
            V((2, 16, 8, 640), BF),
            V((2, 16, 8, 640), BF),
            V((8, 256), BF),
            V((16, 8, 256), BF),
            V((16, 2, 2, 448), F32),
            V((32, 2, 448), F32),
            V((2, 448), BF),
            V((16, 2, 448), BF),
            V((2, 8, 896), F32),
            V((32, 2, 224), F32),
            V((2, 2, 224), F32),
            V((8, 896), BF),
            V((8, 1024), BF),
            V((16, 8, 896), BF),
            V((16, 8, 1024), BF),
            V((32, 128), BF),
            V((32, 128), BF),
            V((16, 32, 224), BF),
            V((16, 32, 224), BF),
            V((16, 4, 224), F32),
            V((16, 4, 224), F32),
            D((13,)),
            D((7,)),
            D((7,)),
            D((11,)),
            D((14,)),
        ],
        compiler_params=pltpu.CompilerParams(
            collective_id=0, has_side_effects=True, vmem_limit_bytes=48 << 20
        ),
        name="decode_layer",
    )(
        *[
            pltpu.with_memory_space_constraint(x, pltpu.HBM)
            for x in (
                lengths, query, jnp.swapaxes(latent_cache, 1, 2), w_uv, w_o.T, residual,
                norm_gain.reshape(56, 128), routes.T, route_weight.T,
                w_gate, w_up, w_down,
            )
        ],
    )


def solution(mesh):
    in_specs = (
        P("ctx", "req"),
        P("req", "ctx", None),
        P("req", "ctx", None),
        P("req"),
        P("ctx", None, None),
        P("ctx", "req"),
        P(),
        P(),
        P(),
        P("req", "ctx", None),
        P("req", "ctx", None),
        P("req", "ctx", None),
    )
    return jax.shard_map(
        local, mesh=mesh, in_specs=in_specs, out_specs=P("req", "ctx"), check_vma=False
    )
```

```python
import jax
import jax.numpy as jnp
from jax import lax
from jax.experimental import pallas as pl
from jax.experimental.pallas import tpu as pltpu
from jax.sharding import PartitionSpec as P

MESH = pl.DeviceIdType.MESH
SCALE = 192.0 ** (-0.5)
NEG = -1e30
EPS = 1e-06
BF = jnp.bfloat16
F32 = jnp.float32
NZ = 16
NC = 32
NCHIP = 16
FAR = (10, 2, 8, 9, 11, 6, 14, 1, 3, 4, 12, 5, 7, 13, 15)
ZORD = (0, 1, 15, 2, 14, 3, 13, 4, 12, 5, 11, 6, 10, 7, 9, 8)
PAIRS = ((0, 1, 7, 2), (6, 3, 5, 4))
ZFAR = (8, 7, 9, 6, 10, 5, 11, 4, 12, 3, 13, 2, 14, 1, 15)


def dot(a, b):
    return jnp.dot(a, b, preferred_element_type=F32)


def dot_t(a, b):
    return lax.dot_general(a, b, (((1,), (1,)), ((), ())), preferred_element_type=F32)


def iota(shape, axis):
    return lax.broadcasted_iota(jnp.int32, shape, axis)


def body(
    lens_hbm, q_hbm, cache_hbm, wuv_hbm, wo_hbm, res_hbm, gain_hbm, routes_hbm, rw_hbm,
    wg_hbm, wu_hbm, wd_hbm,
    out_ref,
    lens, qin, cbuf, wuv, wo, res, gain, routes, rw, table, gain8, gu, wd, wdp,
    qs, qbuf, osend, obuf, vs, vbuf, fs, fbuf, gs, gbuf, mid8, mids, midbuf, xs, xs2, xbuf, xbuf2,
    hs, hb, isend, ibuf, js, jbuf,
    loc, sib_s, sib_r, snd, rcv, greet,
):
    z = lax.axis_index("req")
    c = lax.axis_index("ctx")
    core = lax.rem(c, 2)
    chip = c // 2
    sib = c + 1 - 2 * core

    def chip_at(s):
        x = lax.rem(chip // 4 + s // 4, 4)
        y = lax.rem(lax.rem(chip, 4) + s % 4, 4)
        return x * 4 + y

    def back(s):
        return ((4 - s // 4) % 4) * 4 + (4 - s % 4) % 4

    barrier = pltpu.get_barrier_semaphore()
    near_z = (3, 13, 2, 14, 1, 15)
    for s in near_z:
        pl.semaphore_signal(
            barrier, inc=1, device_id=(lax.rem(z + s, NZ), c), device_id_type=MESH
        )
    for s in FAR:
        pl.semaphore_signal(
            barrier, inc=1, device_id=(z, chip_at(s) * 2 + core), device_id_type=MESH
        )
    pl.semaphore_signal(barrier, inc=1, device_id=(z, sib), device_id_type=MESH)

    def pass_on(i):
        for s in near_z:
            pl.semaphore_signal(
                greet.at[i], inc=1, device_id=(lax.rem(z + s, NZ), c), device_id_type=MESH
            )

    todo = {}

    def begin(name, copy):
        copy.start()
        todo[name] = copy.wait

    def wait(*names):
        for name in names:
            todo.pop(name)()

    def drain(ref, sem):
        pltpu.make_async_copy(ref, ref, sem).wait()

    own, other = pl.ds(0, 512), pl.ds(512, 512)
    first = pl.ds(pl.multiple_of(64 * core, 64), 64)
    second = pl.ds(pl.multiple_of(128 + 64 * core, 64), 64)
    for i, (name, src, dst) in enumerate((
        ("q", q_hbm, qin),
        ("cache0", cache_hbm.at[0], cbuf.at[0, :, own]),
        ("cache1", cache_hbm.at[1], cbuf.at[1, :, own]),
        ("gain", gain_hbm, gain),
        ("routes", routes_hbm, routes),
        ("rw", rw_hbm, rw),
        ("res", res_hbm, res),
        ("wuv", wuv_hbm, wuv),
        ("wo", wo_hbm, wo),
        ("wg", wg_hbm.at[0], gu.at[first]),
        ("wu", wu_hbm.at[0], gu.at[second]),
        ("wd", wd_hbm.at[0], wd.at[first]),
        ("lens", lens_hbm, lens),
    )):
        begin(name, pltpu.make_async_copy(src, dst, loc.at[i]))

    def remote(src, dst, send, recv, dev):
        return pltpu.make_async_remote_copy(
            src_ref=src, dst_ref=dst, send_sem=send, recv_sem=recv,
            device_id=dev, device_id_type=MESH,
        )

    def twin(i, name, src, dst):
        copy = remote(src, dst, sib_s.at[i], sib_r.at[i], (z, sib))
        copy.start()
        todo[name] = copy.wait_recv
        todo[name + "_sent"] = copy.wait_send

    def sent(i, ref):
        todo["sent%d" % i] = lambda: drain(ref, snd.at[i])

    wait("q")
    for r in range(2):
        rows = jnp.concatenate(
            [qin[2 * r].astype(F32), qin[2 * r + 1].astype(F32)], axis=0
        ).astype(BF)
        qs[r] = rows
        qbuf[r, 0] = rows
    pl.semaphore_wait(barrier, len(near_z) + NCHIP)
    for r in range(2):
        twin(5 + r, "twin%d" % r, cache_hbm.at[r], cbuf.at[r, :, other])
        for s in FAR:
            remote(
                qs.at[r], qbuf.at[r, back(s)], snd.at[0], rcv.at[0 if r == 0 else 11],
                (z, chip_at(s) * 2 + core),
            ).start()
    sent(0, qbuf.at[:, pl.ds(0, 15)])
    pass_on(0)
    twin(1, "wg2", wg_hbm.at[0], gu.at[first])
    twin(2, "wu2", wu_hbm.at[0], gu.at[second])
    twin(3, "wd2", wd_hbm.at[0], wd.at[first])

    wait("gain", "routes", "rw")
    g = gain[...].astype(F32)
    for i in range(56):
        m, j = i // 7, i % 7
        table[m, :, 128 * j : 128 * j + 128] = jnp.broadcast_to(g[i : i + 1], (2, 128))

    def pair(far, j):
        return lax.rem(z // 2 + PAIRS[far][j], 8)

    for far in range(2):
        for j in range(4):
            gain8[far, 2 * j : 2 * j + 2] = table[pair(far, j)]
    match = jnp.where(routes[...] == z, 1.0, 0.0)
    coef = jnp.sum(match * rw[...], axis=0, keepdims=True)
    row = iota((128, 64), 0)
    token = 4 * (row // 8) + 2 * core + lax.rem(row, 2)
    pick = (token == iota((128, 64), 1)) & (lax.rem(row, 8) < 2)
    coefs = jnp.sum(jnp.where(pick, coef, 0.0), axis=1, keepdims=True)
    match8 = jnp.broadcast_to(jnp.sum(match, axis=0, keepdims=True), (8, 64)).astype(BF)
    i64, j64 = iota((64, 64), 0), iota((64, 64), 1)
    rank8 = dot(match8, jnp.where(i64 < j64, 1.0, 0.0).astype(BF)).astype(BF)
    pick = jnp.where(pick, 1.0, 0.0).astype(BF)
    fill = (dot_t(match8, pick)[:1] > 0.5) & (
        dot_t(rank8, pick)[:1] == iota((32, 128), 0).astype(F32)
    )
    fill = jnp.where(fill, 1.0, 0.0).astype(BF)
    named = dot_t(jnp.where(i64 == j64, 1.0, 0.0).astype(BF), match8)[:, :1]
    ranks = dot_t(jnp.where(j64 < i64, 1.0, 0.0).astype(BF), match8)[:, :1]
    spread = (named > 0.5) & (ranks == iota((64, 32), 1).astype(F32))
    spread = jnp.where(spread, 1.0, 0.0).astype(BF)

    wait("lens")
    row_k = lax.rem(iota((128, 1024), 0) // 4, 2)
    lane_p = iota((128, 1024), 1)
    place = jnp.where(lane_p < 512, c * 512 + lane_p, sib * 512 + lane_p - 512)
    lane_e = iota((128, 128), 1)
    for r in range(2):
        wait("cache%d" % r, "twin%d" % r)
        drain(qbuf.at[r, pl.ds(1, 15)], rcv.at[0 if r == 0 else 11])
        ql = qbuf[r].astype(F32).reshape(128, 576).astype(BF)
        see = place <= lens[r] - 2 + row_k
        score = jnp.where(see, dot(ql, cbuf[r]) * SCALE, NEG)
        peak = jnp.max(score, axis=1, keepdims=True)
        peak = jnp.where(peak > 0.5 * NEG, peak, 0.0)
        raised = jnp.exp(score - peak)
        total = jnp.sum(raised, axis=1, keepdims=True)
        mixed = dot_t(raised.astype(BF), cbuf[r, :512])
        filled = total > 0.0
        safe = jnp.where(filled, total, 1.0)
        part = jnp.where(filled, mixed / safe, 0.0)
        log = jnp.where(filled, peak + jnp.log(safe), NEG)
        hi = log.astype(BF).astype(F32)
        mi = (log - hi).astype(BF).astype(F32)
        lo = log - hi - mi
        tail = jnp.where(
            lane_e == 0, hi, jnp.where(lane_e == 1, mi, jnp.where(lane_e == 2, lo, 0.0))
        )
        osend[r, :, :, :512] = part.reshape(16, 8, 512).astype(BF)
        osend[r, :, :, 512:] = tail.reshape(16, 8, 128).astype(BF)
        for s in FAR:
            remote(
                osend.at[r, s], obuf.at[r, back(s)], snd.at[1 + r], rcv.at[1 + r],
                (z, chip_at(s) * 2 + core),
            ).start()
        obuf[r, 0] = osend[r, 0]
        sent(1 + r, obuf.at[r, pl.ds(0, 15)])

    pl.semaphore_wait(greet.at[0], len(near_z))
    pass_on(1)
    wait("wuv")
    latents = []
    for r in range(2):
        drain(obuf.at[r, pl.ds(1, 15)], rcv.at[1 + r])
        logs = jnp.sum(obuf[r, :, :, 512:].astype(F32), axis=2, keepdims=True)
        top = jnp.max(logs, axis=0, keepdims=True)
        factor = jnp.exp(logs - top)
        numer = jnp.sum(factor * obuf[r, :, :, :512].astype(F32), axis=0)
        latents.append(numer / jnp.sum(factor, axis=0))
    latent = jnp.concatenate(latents, axis=0).astype(BF)
    r8, c16 = iota((8, 16), 0), iota((8, 16), 1)
    halves = [None, None]
    for h in range(4):
        pick = (r8 // 4 == h // 2) & (c16 == 4 * lax.rem(r8, 4) + h)
        rows = dot(jnp.where(pick, 1.0, 0.0).astype(BF), latent).astype(BF)
        val = dot(rows, wuv[h])
        halves[h % 2] = val if halves[h % 2] is None else halves[h % 2] + val
    vrow = jnp.concatenate(halves, axis=1).astype(BF)
    pl.semaphore_wait(greet.at[1], len(near_z))
    vs[...] = vrow
    vbuf[0] = vrow
    for s in ZFAR:
        pos = ZORD.index(NZ - s)
        remote(
            vs, vbuf.at[pos], snd.at[3], rcv.at[3 if pos < 12 else 9],
            (lax.rem(z + s, NZ), c),
        ).start()
    sent(3, vbuf.at[pl.ds(0, 15)])

    wait("wo")
    for lo, n in ((0, 12), (12, 4)):
        if lo == 0:
            drain(vbuf.at[pl.ds(1, 11)], rcv.at[3])
        else:
            drain(vbuf.at[pl.ds(12, 4)], rcv.at[9])
        vals = vbuf[lo : lo + n].astype(F32).reshape(8 * n, 256).astype(BF)
        y0 = dot_t(vals, wo[:, :256])
        y1 = dot_t(vals, wo[:, 256:])
        y = (y0 + pltpu.roll(y1, 8 * n - 4, 0)).reshape(n, 8, 448)
        fs[lo : lo + n, 0] = y[:, 0:2]
        fs[lo : lo + n, 1] = y[:, 2:4]
        for pos in range(lo, lo + n):
            for k in range(2):
                dst = 2 * lax.rem(z + ZORD[pos], NZ) + k

                @pl.when(dst != c)
                def _():
                    remote(
                        fs.at[pos, k], fbuf.at[c], snd.at[4], rcv.at[4], (z, dst)
                    ).start()

                @pl.when(dst == c)
                def _():
                    fbuf[c] = fs[pos, k]
    sent(4, fbuf.at[pl.ds(0, 31)])

    wait("res")
    drain(fbuf.at[pl.ds(0, 31)], rcv.at[4])
    mid = (jnp.sum(fbuf[...], axis=0) + res[...].astype(F32)).astype(BF)
    gs[...] = mid
    for s in ZFAR:
        near = [(0 - (s + k) // 2) % 8 in PAIRS[0] for k in range(2)]
        sem = 5 if all(near) else 12
        if any(near) and not all(near):
            even = lax.rem(z, 2) == 0
            sem = jnp.where(even, 5 if near[0] else 12, 5 if near[1] else 12)
        remote(
            gs, gbuf.at[z], snd.at[5], rcv.at[sem], (lax.rem(z + s, NZ), c)
        ).start()
    gbuf[z] = mid
    sent(5, gbuf.at[pl.ds(0, 15)])

    wait("wd", "wd2")
    for k in range(2):
        @pl.when(core == k)
        def _():
            for i in range(NCHIP):
                at = 448 * i + 224 * k
                wdp[i, :, :224] = wd[:, at : at + 224]

    lane_w = iota((8, 128), 1)
    sq = jnp.zeros((8, 1), F32)
    for far in range(2):
        if far == 0:
            drain(gbuf.at[pl.ds(0, 7)], rcv.at[5])
        else:
            drain(gbuf.at[pl.ds(0, 8)], rcv.at[12])
        for j in range(4):
            for b in range(2):
                mid8[far, 2 * j : 2 * j + 2, 448 * b : 448 * b + 448] = gbuf[
                    2 * pair(far, j) + b
                ].astype(F32)
        m = mid8[far]
        sq = sq + jnp.sum(m * m, axis=1, keepdims=True)
        gained = (m * gain8[far]).astype(BF)
        if far == 0:
            src, dst, i = xs, xbuf, 6
        else:
            sq = sq + pltpu.roll(sq, 2, 0)
            sq = sq + pltpu.roll(sq, 4, 0)
            norm = lax.rsqrt(sq * (1.0 / 7168.0) + EPS)
            src, dst, i = xs2, xbuf2, 10
            hi = norm.astype(BF).astype(F32)
            mi = (norm - hi).astype(BF).astype(F32)
            tail = jnp.where(
                lane_w == 0,
                hi,
                jnp.where(lane_w == 1, mi, jnp.where(lane_w == 2, norm - hi - mi, 0.0)),
            ).astype(BF)
            gained = jnp.concatenate([gained, tail], axis=1)
        src[...] = gained
        for s in FAR:
            remote(
                src, dst.at[chip], snd.at[i], rcv.at[6 if far == 0 else 13],
                (z, chip_at(s) * 2 + core),
            ).start()
        dst[chip] = gained
        sent(i, dst.at[pl.ds(0, 15)])

    @pl.when(chip == z)
    def _():
        for far in range(2):
            for j in range(4):
                for d in range(4):
                    mids[4 * pair(far, j) + d] = mid8[
                        far, 2 * j : 2 * j + 2, 224 * d : 224 * d + 224
                    ]

        @pl.loop(1, NC)
        def _(s):
            dst = lax.rem(c + s, NC)
            remote(
                mids.at[dst], midbuf.at[core], snd.at[9], rcv.at[10], (z, dst)
            ).start()

        midbuf[core] = mids[c]

    wait("wg", "wu", "wg2", "wu2")
    row_j = lax.rem(iota((128, 256), 0), 8) // 2
    both = jnp.zeros((128, 256), F32)
    for far in range(2):
        if far == 0:
            drain(xbuf.at[pl.ds(0, 15)], rcv.at[6])
            x = xbuf[...].astype(F32)
        else:
            drain(xbuf2.at[pl.ds(0, 15)], rcv.at[13])
            x = xbuf2[...].astype(F32)
        x = x.reshape(128, 896 + 128 * far)
        if far:
            norm = jnp.sum(x[:, 896:], axis=1, keepdims=True)
        x = x[:, :896].astype(BF)
        for j in range(4):
            at = pl.multiple_of(896 * pair(far, j), 128)
            part = dot_t(x, gu[:, pl.ds(at, 896)])
            both = both + jnp.where(row_j == j, part, 0.0)
    both = both + pltpu.roll(both, 126, 0)
    both = (both + pltpu.roll(both, 124, 0)) * norm
    gate, up = both[:, :128], both[:, 128:]
    hidden = gate / (1.0 + jnp.exp(-gate)) * up * coefs
    keep = lax.rem(iota((128, 128), 0), 8) < 2
    hidden = jnp.where(keep, hidden, 0.0).astype(BF)
    short = dot(fill, hidden)
    hs[...] = short.astype(BF)
    twin(4, "hidden", hs, hb)
    wait("hidden")
    short = (short + hb[...].astype(F32)).astype(BF)
    order = FAR + (0,)
    for lo in range(0, NCHIP, 8):
        for s in order[lo : lo + 8]:
            isend[s] = dot(short, wdp[chip_at(s)])[:, :224].astype(BF)
        for s in order[lo : lo + 8]:
            if s:
                remote(
                    isend.at[s], ibuf.at[back(s)], snd.at[7], rcv.at[7],
                    (z, chip_at(s) * 2 + core),
                ).start()
    ibuf[0] = isend[0]
    sent(7, ibuf.at[pl.ds(0, 15)])

    drain(ibuf.at[pl.ds(1, 15)], rcv.at[7])
    acc = jnp.sum(ibuf[...].astype(F32), axis=0)
    hi = acc.astype(BF)
    mi = (acc - hi.astype(F32)).astype(BF)
    lo = (acc - hi.astype(F32) - mi.astype(F32)).astype(BF)
    acc = dot(spread, hi) + dot(spread, mi) + dot(spread, lo)
    for p in range(NZ):
        js[p] = acc[4 * p : 4 * p + 4]
    for s in ZFAR:
        dst = lax.rem(z + s, NZ)
        remote(js.at[dst], jbuf.at[z], snd.at[8], rcv.at[8], (dst, c)).start()
    jbuf[z] = js[z]
    drain(jbuf.at[pl.ds(0, 15)], rcv.at[8])
    last = jnp.sum(jbuf[...], axis=0)

    @pl.when(chip == z)
    def _():
        drain(midbuf.at[0], rcv.at[10])
        drain(mids.at[pl.ds(0, 31)], snd.at[9])

    @pl.when(chip != z)
    def _():
        drain(midbuf, rcv.at[10])

    mid = jnp.concatenate([midbuf[0], midbuf[1]], axis=0)
    out_ref[...] = (last + mid).astype(BF)
    sent(8, jbuf.at[pl.ds(0, 15)])
    wait(*list(todo))


def local(
    residual, query, latent_cache, lengths, w_uv, w_o, norm_gain, routes, route_weight,
    w_gate, w_up, w_down,
):
    hbm = pl.BlockSpec(memory_space=pltpu.HBM)
    vmem = pl.BlockSpec(memory_space=pltpu.VMEM)
    V = pltpu.VMEM
    D = pltpu.SemaphoreType.DMA
    return pl.pallas_call(
        body,
        out_shape=jax.ShapeDtypeStruct((4, 224), BF),
        in_specs=[hbm] * 12,
        out_specs=vmem,
        scratch_shapes=[
            pltpu.SMEM((2,), jnp.int32),
            V((4, 4, 576), BF),
            V((2, 576, 1024), BF),
            V((4, 512, 128), BF),
            V((448, 512), BF),
            V((2, 448), BF),
            V((56, 128), BF),
            V((4, 64), jnp.int32),
            V((4, 64), F32),
            V((8, 2, 896), F32),
            V((2, 8, 896), F32),
            V((256, 7168), BF),
            V((128, 7168), BF),
            V((16, 128, 256), BF),
            V((2, 8, 576), BF),
            V((2, 16, 8, 576), BF),
            V((2, 16, 8, 640), BF),
            V((2, 16, 8, 640), BF),
            V((8, 256), BF),
            V((16, 8, 256), BF),
            V((16, 2, 2, 448), F32),
            V((32, 2, 448), F32),
            V((2, 448), BF),
            V((16, 2, 448), BF),
            V((2, 8, 896), F32),
            V((32, 2, 224), F32),
            V((2, 2, 224), F32),
            V((8, 896), BF),
            V((8, 1024), BF),
            V((16, 8, 896), BF),
            V((16, 8, 1024), BF),
            V((32, 128), BF),
            V((32, 128), BF),
            V((16, 32, 224), BF),
            V((16, 32, 224), BF),
            V((16, 4, 224), F32),
            V((16, 4, 224), F32),
            D((13,)),
            D((7,)),
            D((7,)),
            D((11,)),
            D((14,)),
            pltpu.SemaphoreType.REGULAR((2,)),
        ],
        compiler_params=pltpu.CompilerParams(
            collective_id=0, has_side_effects=True, vmem_limit_bytes=48 << 20
        ),
        name="decode_layer",
    )(
        *[
            pltpu.with_memory_space_constraint(x, pltpu.HBM)
            for x in (
                lengths, query, jnp.swapaxes(latent_cache, 1, 2), w_uv, w_o.T, residual,
                norm_gain.reshape(56, 128), routes.T, route_weight.T,
                w_gate, w_up, w_down,
            )
        ],
    )


def solution(mesh):
    in_specs = (
        P("ctx", "req"),
        P("req", "ctx", None),
        P("req", "ctx", None),
        P("req"),
        P("ctx", None, None),
        P("ctx", "req"),
        P(),
        P(),
        P(),
        P("req", "ctx", None),
        P("req", "ctx", None),
        P("req", "ctx", None),
    )
    return jax.shard_map(
        local, mesh=mesh, in_specs=in_specs, out_specs=P("req", "ctx"), check_vma=False
    )
```

```python
import jax
import jax.numpy as jnp
from jax import lax
from jax.experimental import pallas as pl
from jax.experimental.pallas import tpu as pltpu
from jax.sharding import PartitionSpec as P

MESH = pl.DeviceIdType.MESH
SCALE = 192.0 ** (-0.5)
NEG = -1e30
EPS = 1e-06
BF = jnp.bfloat16
F32 = jnp.float32
NZ = 16
NC = 32
NCHIP = 16
FAR = (10, 2, 8, 9, 11, 6, 14, 1, 3, 4, 12, 5, 7, 13, 15)
ZORD = (0, 1, 15, 2, 14, 3, 13, 4, 12, 5, 11, 6, 10, 7, 9, 8)
PAIRS = ((0, 1, 7, 2), (6, 3, 5, 4))
ZFAR = (8, 7, 9, 6, 10, 5, 11, 4, 12, 3, 13, 2, 14, 1, 15)


def dot(a, b):
    return jnp.dot(a, b, preferred_element_type=F32)


def dot_t(a, b):
    return lax.dot_general(a, b, (((1,), (1,)), ((), ())), preferred_element_type=F32)


def iota(shape, axis):
    return lax.broadcasted_iota(jnp.int32, shape, axis)


def body(
    lens_hbm, q_hbm, cache_hbm, wuv_hbm, wo_hbm, res_hbm, gain_hbm, routes_hbm, rw_hbm,
    wg_hbm, wu_hbm, wd_hbm,
    out_ref,
    lens, qin, cbuf, wuv, wo, res, gain, routes, rw, table, gain8, gu, wd, wdp,
    qs, qbuf, osend, obuf, vs, vbuf, fs, fbuf, gs, gbuf, mid8, mids, midbuf, xs, xs2, xbuf, xbuf2,
    hs, hb, isend, ibuf, js, jbuf,
    loc, sib_s, sib_r, snd, rcv, greet,
):
    z = lax.axis_index("req")
    c = lax.axis_index("ctx")
    core = lax.rem(c, 2)
    chip = c // 2
    sib = c + 1 - 2 * core

    def chip_at(s):
        x = lax.rem(chip // 4 + s // 4, 4)
        y = lax.rem(lax.rem(chip, 4) + s % 4, 4)
        return x * 4 + y

    def back(s):
        return ((4 - s // 4) % 4) * 4 + (4 - s % 4) % 4

    barrier = pltpu.get_barrier_semaphore()
    near_z = (3, 13, 2, 14, 1, 15)
    for s in FAR:
        pl.semaphore_signal(
            barrier, inc=1, device_id=(z, chip_at(s) * 2 + core), device_id_type=MESH
        )
    for s in near_z:
        pl.semaphore_signal(
            barrier, inc=1, device_id=(lax.rem(z + s, NZ), c), device_id_type=MESH
        )
    pl.semaphore_signal(barrier, inc=1, device_id=(z, sib), device_id_type=MESH)

    def pass_on(i):
        for s in near_z:
            pl.semaphore_signal(
                greet.at[i], inc=1, device_id=(lax.rem(z + s, NZ), c), device_id_type=MESH
            )

    todo = {}

    def begin(name, copy):
        copy.start()
        todo[name] = copy.wait

    def wait(*names):
        for name in names:
            todo.pop(name)()

    def drain(ref, sem):
        pltpu.make_async_copy(ref, ref, sem).wait()

    own, other = pl.ds(0, 512), pl.ds(512, 512)
    first = pl.ds(pl.multiple_of(64 * core, 64), 64)
    second = pl.ds(pl.multiple_of(128 + 64 * core, 64), 64)
    for i, (name, src, dst) in enumerate((
        ("q", q_hbm, qin),
        ("cache0", cache_hbm.at[0], cbuf.at[0, :, own]),
        ("cache1", cache_hbm.at[1], cbuf.at[1, :, own]),
        ("gain", gain_hbm, gain),
        ("routes", routes_hbm, routes),
        ("rw", rw_hbm, rw),
        ("res", res_hbm, res),
        ("wuv", wuv_hbm, wuv),
        ("wo", wo_hbm, wo),
        ("wg", wg_hbm.at[0], gu.at[first]),
        ("wu", wu_hbm.at[0], gu.at[second]),
        ("wd", wd_hbm.at[0], wd.at[first]),
        ("lens", lens_hbm, lens),
    )):
        begin(name, pltpu.make_async_copy(src, dst, loc.at[i]))

    def remote(src, dst, send, recv, dev):
        return pltpu.make_async_remote_copy(
            src_ref=src, dst_ref=dst, send_sem=send, recv_sem=recv,
            device_id=dev, device_id_type=MESH,
        )

    def twin(i, name, src, dst):
        copy = remote(src, dst, sib_s.at[i], sib_r.at[i], (z, sib))
        copy.start()
        todo[name] = copy.wait_recv
        todo[name + "_sent"] = copy.wait_send

    def sent(i, ref):
        todo["sent%d" % i] = lambda: drain(ref, snd.at[i])

    wait("q")
    for r in range(2):
        rows = jnp.concatenate(
            [qin[2 * r].astype(F32), qin[2 * r + 1].astype(F32)], axis=0
        ).astype(BF)
        qs[r] = rows
        qbuf[r, 0] = rows
    pl.semaphore_wait(barrier, len(near_z) + NCHIP)
    for r in range(2):
        twin(5 + r, "twin%d" % r, cache_hbm.at[r], cbuf.at[r, :, other])
        for s in FAR:
            remote(
                qs.at[r], qbuf.at[r, back(s)], snd.at[0], rcv.at[0 if r == 0 else 11],
                (z, chip_at(s) * 2 + core),
            ).start()
    sent(0, qbuf.at[:, pl.ds(0, 15)])
    pass_on(0)
    twin(1, "wg2", wg_hbm.at[0], gu.at[first])
    twin(2, "wu2", wu_hbm.at[0], gu.at[second])
    twin(3, "wd2", wd_hbm.at[0], wd.at[first])

    wait("gain", "routes", "rw")
    g = gain[...].astype(F32)
    for i in range(56):
        m, j = i // 7, i % 7
        table[m, :, 128 * j : 128 * j + 128] = jnp.broadcast_to(g[i : i + 1], (2, 128))

    def pair(far, j):
        return lax.rem(z // 2 + PAIRS[far][j], 8)

    for far in range(2):
        for j in range(4):
            gain8[far, 2 * j : 2 * j + 2] = table[pair(far, j)]
    seat = lax.rem(chip - z + 28, NCHIP)
    coef = jnp.sum(jnp.where(routes[...] == z, rw[...], 0.0), axis=0, keepdims=True)
    row = iota((128, 64), 0)
    token = 4 * lax.rem(row // 8 + z + 4, NCHIP) + 2 * core + lax.rem(row, 2)
    pick = (token == iota((128, 64), 1)) & (lax.rem(row, 8) < 2)
    coefs = jnp.sum(jnp.where(pick, coef, 0.0), axis=1, keepdims=True)

    wait("lens")
    row_k = lax.rem(iota((128, 1024), 0) // 4, 2)
    lane_p = iota((128, 1024), 1)
    place = jnp.where(lane_p < 512, c * 512 + lane_p, sib * 512 + lane_p - 512)
    lane_e = iota((128, 128), 1)
    for r in range(2):
        wait("cache%d" % r, "twin%d" % r)
        drain(qbuf.at[r, pl.ds(1, 15)], rcv.at[0 if r == 0 else 11])
        ql = qbuf[r].astype(F32).reshape(128, 576).astype(BF)
        see = place <= lens[r] - 2 + row_k
        score = jnp.where(see, dot(ql, cbuf[r]) * SCALE, NEG)
        peak = jnp.max(score, axis=1, keepdims=True)
        peak = jnp.where(peak > 0.5 * NEG, peak, 0.0)
        raised = jnp.exp(score - peak)
        total = jnp.sum(raised, axis=1, keepdims=True)
        mixed = dot_t(raised.astype(BF), cbuf[r, :512])
        filled = total > 0.0
        safe = jnp.where(filled, total, 1.0)
        part = jnp.where(filled, mixed / safe, 0.0)
        log = jnp.where(filled, peak + jnp.log(safe), NEG)
        hi = log.astype(BF).astype(F32)
        mi = (log - hi).astype(BF).astype(F32)
        lo = log - hi - mi
        tail = jnp.where(
            lane_e == 0, hi, jnp.where(lane_e == 1, mi, jnp.where(lane_e == 2, lo, 0.0))
        )
        osend[r, :, :, :512] = part.reshape(16, 8, 512).astype(BF)
        osend[r, :, :, 512:] = tail.reshape(16, 8, 128).astype(BF)
        for s in FAR:
            remote(
                osend.at[r, s], obuf.at[r, back(s)], snd.at[1 + r], rcv.at[1 + r],
                (z, chip_at(s) * 2 + core),
            ).start()
        obuf[r, 0] = osend[r, 0]
        sent(1 + r, obuf.at[r, pl.ds(0, 15)])

    pl.semaphore_wait(greet.at[0], len(near_z))
    pass_on(1)
    wait("wuv")
    latents = []
    for r in range(2):
        drain(obuf.at[r, pl.ds(1, 15)], rcv.at[1 + r])
        logs = jnp.sum(obuf[r, :, :, 512:].astype(F32), axis=2, keepdims=True)
        top = jnp.max(logs, axis=0, keepdims=True)
        factor = jnp.exp(logs - top)
        numer = jnp.sum(factor * obuf[r, :, :, :512].astype(F32), axis=0)
        latents.append(numer / jnp.sum(factor, axis=0))
    latent = jnp.concatenate(latents, axis=0).astype(BF)
    r8, c16 = iota((8, 16), 0), iota((8, 16), 1)
    halves = [None, None]
    for h in range(4):
        pick = (r8 // 4 == h // 2) & (c16 == 4 * lax.rem(r8, 4) + h)
        rows = dot(jnp.where(pick, 1.0, 0.0).astype(BF), latent).astype(BF)
        val = dot(rows, wuv[h])
        halves[h % 2] = val if halves[h % 2] is None else halves[h % 2] + val
    vrow = jnp.concatenate(halves, axis=1).astype(BF)
    pl.semaphore_wait(greet.at[1], len(near_z))
    vs[...] = vrow
    vbuf[0] = vrow
    for s in ZFAR:
        pos = ZORD.index(NZ - s)
        remote(
            vs, vbuf.at[pos], snd.at[3], rcv.at[3 if pos < 7 else 9 if pos < 11 else 16],
            (lax.rem(z + s, NZ), c),
        ).start()
    sent(3, vbuf.at[pl.ds(0, 15)])

    wait("wo")
    for lo, n, sem in ((0, 7, 3), (7, 4, 9), (11, 5, 16)):
        own_block = 1 if lo == 0 else 0
        drain(vbuf.at[pl.ds(lo + own_block, n - own_block)], rcv.at[sem])
        vals = vbuf[lo : lo + n].astype(F32).reshape(8 * n, 256).astype(BF)
        y0 = dot_t(vals, wo[:, :256])
        y1 = dot_t(vals, wo[:, 256:])
        y = (y0 + pltpu.roll(y1, 8 * n - 4, 0)).reshape(n, 8, 448)
        fs[lo : lo + n, 0] = y[:, 0:2]
        fs[lo : lo + n, 1] = y[:, 2:4]
        for pos in range(lo, lo + n):
            for k in range(2):
                dst = 2 * lax.rem(z + ZORD[pos], NZ) + k

                @pl.when(dst != c)
                def _():
                    remote(
                        fs.at[pos, k], fbuf.at[c], snd.at[4], rcv.at[4], (z, dst)
                    ).start()

                @pl.when(dst == c)
                def _():
                    fbuf[c] = fs[pos, k]
    sent(4, fbuf.at[pl.ds(0, 31)])

    wait("res")
    drain(fbuf.at[pl.ds(0, 31)], rcv.at[4])
    mid = (jnp.sum(fbuf[...], axis=0) + res[...].astype(F32)).astype(BF)
    gs[...] = mid
    for s in ZFAR:
        near = [(0 - (s + k) // 2) % 8 in PAIRS[0] for k in range(2)]
        sem = 5 if all(near) else 12
        if any(near) and not all(near):
            even = lax.rem(z, 2) == 0
            sem = jnp.where(even, 5 if near[0] else 12, 5 if near[1] else 12)
        remote(
            gs, gbuf.at[z], snd.at[5], rcv.at[sem], (lax.rem(z + s, NZ), c)
        ).start()
    gbuf[z] = mid
    sent(5, gbuf.at[pl.ds(0, 15)])

    wait("wd", "wd2")
    for k in range(2):
        @pl.when(core == k)
        def _():
            for i in range(NCHIP):
                at = 448 * i + 224 * k
                wdp[i, :, :224] = wd[:, at : at + 224]

    lane_w = iota((8, 128), 1)
    sq = jnp.zeros((8, 1), F32)
    arrival = [jnp.where(seat < 8, 6, 14), jnp.where(seat < 8, 13, 15)]
    for far in range(2):
        if far == 0:
            drain(gbuf.at[pl.ds(0, 7)], rcv.at[5])
        else:
            drain(gbuf.at[pl.ds(0, 8)], rcv.at[12])
        for j in range(4):
            for b in range(2):
                mid8[far, 2 * j : 2 * j + 2, 448 * b : 448 * b + 448] = gbuf[
                    2 * pair(far, j) + b
                ].astype(F32)
        m = mid8[far]
        sq = sq + jnp.sum(m * m, axis=1, keepdims=True)
        gained = (m * gain8[far]).astype(BF)
        if far == 0:
            src, dst, i = xs, xbuf, 6
        else:
            sq = sq + pltpu.roll(sq, 2, 0)
            sq = sq + pltpu.roll(sq, 4, 0)
            norm = lax.rsqrt(sq * (1.0 / 7168.0) + EPS)
            src, dst, i = xs2, xbuf2, 10
            hi = norm.astype(BF).astype(F32)
            mi = (norm - hi).astype(BF).astype(F32)
            tail = jnp.where(
                lane_w == 0,
                hi,
                jnp.where(lane_w == 1, mi, jnp.where(lane_w == 2, norm - hi - mi, 0.0)),
            ).astype(BF)
            gained = jnp.concatenate([gained, tail], axis=1)
        src[...] = gained
        for s in FAR:
            remote(
                src, dst.at[seat], snd.at[i], rcv.at[arrival[far]],
                (z, chip_at(s) * 2 + core),
            ).start()
        dst[seat] = gained
        sent(i, dst.at[pl.ds(0, 15)])

    @pl.when(chip == z)
    def _():
        for far in range(2):
            for j in range(4):
                for d in range(4):
                    mids[4 * pair(far, j) + d] = mid8[
                        far, 2 * j : 2 * j + 2, 224 * d : 224 * d + 224
                    ]

        @pl.loop(1, NC)
        def _(s):
            dst = lax.rem(c + s, NC)
            remote(
                mids.at[dst], midbuf.at[core], snd.at[9], rcv.at[10], (z, dst)
            ).start()

        midbuf[core] = mids[c]

    wait("wg", "wu", "wg2", "wu2")
    row_j = lax.rem(iota((64, 256), 0), 8) // 2

    def arrived(buf, part, sem):
        mine = seat // 8 == part

        @pl.when(mine)
        def _():
            drain(buf.at[pl.ds(8 * part, 7)], sem)

        @pl.when(jnp.logical_not(mine))
        def _():
            drain(buf.at[pl.ds(8 * part, 8)], sem)

    def project(x, far):
        total = jnp.zeros((64, 256), F32)
        for j in range(4):
            at = pl.multiple_of(896 * pair(far, j), 128)
            total = total + jnp.where(row_j == j, dot_t(x, gu[:, pl.ds(at, 896)]), 0.0)
        return total

    sums = []
    for part in range(2):
        arrived(xbuf, part, rcv.at[6 if part == 0 else 14])
        x = xbuf[8 * part : 8 * part + 8].astype(F32).reshape(64, 896).astype(BF)
        sums.append(project(x, 0))
    keep = lax.rem(iota((64, 128), 0), 8) < 2
    r16, c64 = iota((16, 64), 0), iota((16, 64), 1)
    squeeze = jnp.where(c64 == 8 * (r16 // 2) + lax.rem(r16, 2), 1.0, 0.0).astype(BF)
    order = FAR + (0,)
    for part in range(2):
        arrived(xbuf2, part, rcv.at[13 if part == 0 else 15])
        x = xbuf2[8 * part : 8 * part + 8].astype(F32).reshape(64, 1024)
        norm = jnp.sum(x[:, 896:], axis=1, keepdims=True)
        both = sums[part] + project(x[:, :896].astype(BF), 1)
        both = both + pltpu.roll(both, 62, 0)
        both = (both + pltpu.roll(both, 60, 0)) * norm
        gate, up = both[:, :128], both[:, 128:]
        hidden = gate / (1.0 + jnp.exp(-gate)) * up * coefs[64 * part : 64 * part + 64]
        hidden = jnp.where(keep, hidden, 0.0).astype(BF)
        short = dot(squeeze, hidden).astype(BF)
        hs[part] = short
        twin(4 * part, "hidden%d" % part, hs.at[part], hb.at[part, core])
        hb[part, core] = short
        wait("hidden%d" % part)
        short = hb[part].reshape(32, 128)
        for lo in range(0, NCHIP, 8):
            for s in order[lo : lo + 8]:
                isend[part, s] = dot(short, wdp[chip_at(s)])[:, :224].astype(BF)
            for s in order[lo : lo + 8]:
                if s:
                    remote(
                        isend.at[part, s], ibuf.at[part, back(s)],
                        snd.at[7 if part == 0 else 11], rcv.at[7 if part == 0 else 17],
                        (z, chip_at(s) * 2 + core),
                    ).start()
        ibuf[part, 0] = isend[part, 0]
        sent(7 if part == 0 else 11, ibuf.at[part, pl.ds(0, 15)])

    for part, seats in enumerate(((4, 3, 5, 2, 6, 1, 7, 0), (8, 9, 15, 10, 14, 11, 13))):
        drain(ibuf.at[part, pl.ds(1, 15)], rcv.at[7 if part == 0 else 17])
        acc = jnp.sum(ibuf[part].astype(F32), axis=0)
        for i in range(8):
            for k in range(2):
                at = 16 * k + 2 * i
                js[8 * part + i, 2 * k : 2 * k + 2] = acc[at : at + 2]
        for i in seats:
            remote(
                js.at[i], jbuf.at[z], snd.at[8], rcv.at[8], (lax.rem(z + 4 + i, NZ), c)
            ).start()
    jbuf[z] = js[12]
    drain(jbuf.at[pl.ds(0, 15)], rcv.at[8])
    last = jnp.sum(jbuf[...], axis=0)

    @pl.when(chip == z)
    def _():
        drain(midbuf.at[0], rcv.at[10])
        drain(mids.at[pl.ds(0, 31)], snd.at[9])

    @pl.when(chip != z)
    def _():
        drain(midbuf, rcv.at[10])

    mid = jnp.concatenate([midbuf[0], midbuf[1]], axis=0)
    out_ref[...] = (last + mid).astype(BF)
    sent(8, jbuf.at[pl.ds(0, 15)])
    wait(*list(todo))


def local(
    residual, query, latent_cache, lengths, w_uv, w_o, norm_gain, routes, route_weight,
    w_gate, w_up, w_down,
):
    hbm = pl.BlockSpec(memory_space=pltpu.HBM)
    vmem = pl.BlockSpec(memory_space=pltpu.VMEM)
    V = pltpu.VMEM
    D = pltpu.SemaphoreType.DMA
    return pl.pallas_call(
        body,
        out_shape=jax.ShapeDtypeStruct((4, 224), BF),
        in_specs=[hbm] * 12,
        out_specs=vmem,
        scratch_shapes=[
            pltpu.SMEM((2,), jnp.int32),
            V((4, 4, 576), BF),
            V((2, 576, 1024), BF),
            V((4, 512, 128), BF),
            V((448, 512), BF),
            V((2, 448), BF),
            V((56, 128), BF),
            V((4, 64), jnp.int32),
            V((4, 64), F32),
            V((8, 2, 896), F32),
            V((2, 8, 896), F32),
            V((256, 7168), BF),
            V((128, 7168), BF),
            V((16, 128, 256), BF),
            V((2, 8, 576), BF),
            V((2, 16, 8, 576), BF),
            V((2, 16, 8, 640), BF),
            V((2, 16, 8, 640), BF),
            V((8, 256), BF),
            V((16, 8, 256), BF),
            V((16, 2, 2, 448), F32),
            V((32, 2, 448), F32),
            V((2, 448), BF),
            V((16, 2, 448), BF),
            V((2, 8, 896), F32),
            V((32, 2, 224), F32),
            V((2, 2, 224), F32),
            V((8, 896), BF),
            V((8, 1024), BF),
            V((16, 8, 896), BF),
            V((16, 8, 1024), BF),
            V((2, 16, 128), BF),
            V((2, 2, 16, 128), BF),
            V((2, 16, 32, 224), BF),
            V((2, 16, 32, 224), BF),
            V((16, 4, 224), F32),
            V((16, 4, 224), F32),
            D((13,)),
            D((7,)),
            D((7,)),
            D((12,)),
            D((18,)),
            pltpu.SemaphoreType.REGULAR((2,)),
        ],
        compiler_params=pltpu.CompilerParams(
            collective_id=0, has_side_effects=True, vmem_limit_bytes=48 << 20
        ),
        name="decode_layer",
    )(
        *[
            pltpu.with_memory_space_constraint(x, pltpu.HBM)
            for x in (
                lengths, query, jnp.swapaxes(latent_cache, 1, 2), w_uv, w_o.T, residual,
                norm_gain.reshape(56, 128), routes.T, route_weight.T,
                w_gate, w_up, w_down,
            )
        ],
    )


def solution(mesh):
    in_specs = (
        P("ctx", "req"),
        P("req", "ctx", None),
        P("req", "ctx", None),
        P("req"),
        P("ctx", None, None),
        P("ctx", "req"),
        P(),
        P(),
        P(),
        P("req", "ctx", None),
        P("req", "ctx", None),
        P("req", "ctx", None),
    )
    return jax.shard_map(
        local, mesh=mesh, in_specs=in_specs, out_specs=P("req", "ctx"), check_vma=False
    )
```

```python
import jax
import jax.numpy as jnp
from jax import lax
from jax.experimental import pallas as pl
from jax.experimental.pallas import tpu as pltpu
from jax.sharding import PartitionSpec as P

MESH = pl.DeviceIdType.MESH
SCALE = 192.0 ** (-0.5)
NEG = -1e30
EPS = 1e-06
BF = jnp.bfloat16
F32 = jnp.float32
NZ = 16
NC = 32
NCHIP = 16
FAR = (10, 2, 8, 9, 11, 6, 14, 1, 3, 4, 12, 5, 7, 13, 15)
ZORD = (0, 1, 15, 2, 14, 3, 13, 4, 12, 5, 11, 6, 10, 7, 9, 8)
PAIRS = ((0, 1, 7, 2), (6, 3, 5, 4))
ZFAR = (8, 7, 9, 6, 10, 5, 11, 4, 12, 3, 13, 2, 14, 1, 15)


def dot(a, b):
    return jnp.dot(a, b, preferred_element_type=F32)


def dot_t(a, b):
    return lax.dot_general(a, b, (((1,), (1,)), ((), ())), preferred_element_type=F32)


def iota(shape, axis):
    return lax.broadcasted_iota(jnp.int32, shape, axis)


def body(
    lens_hbm, q_hbm, cache_hbm, wuv_hbm, wo_hbm, res_hbm, gain_hbm, routes_hbm, rw_hbm,
    wg_hbm, wu_hbm, wd_hbm,
    out_ref,
    lens, qin, cbuf, wuv, wo, res, gain, routes, rw, table, gain8, gu, wd, wdp,
    qs, qbuf, osend, obuf, vs, vbuf, fs, fbuf, gs, gbuf, mid8, mids, midbuf, xs, xs2, xbuf, xbuf2,
    hs, hb, isend, ibuf, js, jbuf,
    loc, sib_s, sib_r, snd, rcv, greet,
):
    z = lax.axis_index("req")
    c = lax.axis_index("ctx")
    core = lax.rem(c, 2)
    chip = c // 2
    sib = c + 1 - 2 * core

    def chip_at(s):
        x = lax.rem(chip // 4 + s // 4, 4)
        y = lax.rem(lax.rem(chip, 4) + s % 4, 4)
        return x * 4 + y

    def back(s):
        return ((4 - s // 4) % 4) * 4 + (4 - s % 4) % 4

    barrier = pltpu.get_barrier_semaphore()
    near_z = (3, 13, 2, 14, 1, 15)
    for s in FAR:
        pl.semaphore_signal(
            barrier, inc=1, device_id=(z, chip_at(s) * 2 + core), device_id_type=MESH
        )
    for s in near_z:
        pl.semaphore_signal(
            barrier, inc=1, device_id=(lax.rem(z + s, NZ), c), device_id_type=MESH
        )
    pl.semaphore_signal(barrier, inc=1, device_id=(z, sib), device_id_type=MESH)

    def pass_on(i):
        for s in near_z:
            pl.semaphore_signal(
                greet.at[i], inc=1, device_id=(lax.rem(z + s, NZ), c), device_id_type=MESH
            )

    todo = {}

    def begin(name, copy):
        copy.start()
        todo[name] = copy.wait

    def wait(*names):
        for name in names:
            todo.pop(name)()

    def drain(ref, sem):
        pltpu.make_async_copy(ref, ref, sem).wait()

    own, other = pl.ds(0, 512), pl.ds(512, 512)
    first = pl.ds(pl.multiple_of(64 * core, 64), 64)
    second = pl.ds(pl.multiple_of(128 + 64 * core, 64), 64)
    for i, (name, src, dst) in enumerate((
        ("q", q_hbm, qin),
        ("cache0", cache_hbm.at[0], cbuf.at[0, :, own]),
        ("cache1", cache_hbm.at[1], cbuf.at[1, :, own]),
        ("gain", gain_hbm, gain),
        ("routes", routes_hbm, routes),
        ("rw", rw_hbm, rw),
        ("res", res_hbm, res),
        ("wuv", wuv_hbm, wuv),
        ("wo", wo_hbm, wo),
        ("wg", wg_hbm.at[0], gu.at[first]),
        ("wu", wu_hbm.at[0], gu.at[second]),
        ("wd", wd_hbm.at[0], wd.at[first]),
        ("lens", lens_hbm, lens),
    )):
        begin(name, pltpu.make_async_copy(src, dst, loc.at[i]))

    def remote(src, dst, send, recv, dev):
        return pltpu.make_async_remote_copy(
            src_ref=src, dst_ref=dst, send_sem=send, recv_sem=recv,
            device_id=dev, device_id_type=MESH,
        )

    def twin(i, name, src, dst):
        copy = remote(src, dst, sib_s.at[i], sib_r.at[i], (z, sib))
        copy.start()
        todo[name] = copy.wait_recv
        todo[name + "_sent"] = copy.wait_send

    def sent(i, ref):
        todo["sent%d" % i] = lambda: drain(ref, snd.at[i])

    wait("q")
    for r in range(2):
        rows = jnp.concatenate(
            [qin[2 * r].astype(F32), qin[2 * r + 1].astype(F32)], axis=0
        ).astype(BF)
        qs[r] = rows
        qbuf[r, 0] = rows
    pl.semaphore_wait(barrier, len(near_z) + NCHIP)
    for r in range(2):
        twin(5 + r, "twin%d" % r, cache_hbm.at[r], cbuf.at[r, :, other])
        for s in FAR:
            remote(
                qs.at[r], qbuf.at[r, back(s)], snd.at[0], rcv.at[0 if r == 0 else 11],
                (z, chip_at(s) * 2 + core),
            ).start()
    sent(0, qbuf.at[:, pl.ds(0, 15)])
    pass_on(0)
    twin(1, "wg2", wg_hbm.at[0], gu.at[first])
    twin(2, "wu2", wu_hbm.at[0], gu.at[second])
    twin(3, "wd2", wd_hbm.at[0], wd.at[first])

    wait("gain", "routes", "rw")
    g = gain[...].astype(F32)
    for i in range(56):
        m, j = i // 7, i % 7
        table[m, :, 128 * j : 128 * j + 128] = jnp.broadcast_to(g[i : i + 1], (2, 128))

    def pair(far, j):
        return lax.rem(z // 2 + PAIRS[far][j], 8)

    for far in range(2):
        for j in range(4):
            gain8[far, 2 * j : 2 * j + 2] = table[pair(far, j)]
    seat = lax.rem(chip - z + 28, NCHIP)
    coef = jnp.sum(jnp.where(routes[...] == z, rw[...], 0.0), axis=0, keepdims=True)
    row = iota((128, 64), 0)
    token = 4 * lax.rem(row // 8 + z + 4, NCHIP) + 2 * core + lax.rem(row, 2)
    pick = (token == iota((128, 64), 1)) & (lax.rem(row, 8) < 2)
    coefs = jnp.sum(jnp.where(pick, coef, 0.0), axis=1, keepdims=True)

    wait("lens")
    row_k = lax.rem(iota((128, 1024), 0) // 4, 2)
    lane_p = iota((128, 1024), 1)
    place = jnp.where(lane_p < 512, c * 512 + lane_p, sib * 512 + lane_p - 512)
    lane_e = iota((128, 128), 1)
    for r in range(2):
        wait("cache%d" % r, "twin%d" % r)
        drain(qbuf.at[r, pl.ds(1, 15)], rcv.at[0 if r == 0 else 11])
        ql = qbuf[r].astype(F32).reshape(128, 576).astype(BF)
        see = place <= lens[r] - 2 + row_k
        score = jnp.where(see, dot(ql, cbuf[r]) * SCALE, NEG)
        peak = jnp.max(score, axis=1, keepdims=True)
        peak = jnp.where(peak > 0.5 * NEG, peak, 0.0)
        raised = jnp.exp(score - peak)
        total = jnp.sum(raised, axis=1, keepdims=True)
        mixed = dot_t(raised.astype(BF), cbuf[r, :512])
        filled = total > 0.0
        safe = jnp.where(filled, total, 1.0)
        part = jnp.where(filled, mixed / safe, 0.0)
        log = jnp.where(filled, peak + jnp.log(safe), NEG)
        hi = log.astype(BF).astype(F32)
        mi = (log - hi).astype(BF).astype(F32)
        lo = log - hi - mi
        tail = jnp.where(
            lane_e == 0, hi, jnp.where(lane_e == 1, mi, jnp.where(lane_e == 2, lo, 0.0))
        )
        osend[r, :, :, :512] = part.reshape(16, 8, 512).astype(BF)
        osend[r, :, :, 512:] = tail.reshape(16, 8, 128).astype(BF)
        for s in FAR:
            remote(
                osend.at[r, s], obuf.at[r, back(s)], snd.at[1 + r], rcv.at[1 + r],
                (z, chip_at(s) * 2 + core),
            ).start()
        obuf[r, 0] = osend[r, 0]
        sent(1 + r, obuf.at[r, pl.ds(0, 15)])

    pl.semaphore_wait(greet.at[0], len(near_z))
    pass_on(1)
    wait("wuv")
    latents = []
    for r in range(2):
        drain(obuf.at[r, pl.ds(1, 15)], rcv.at[1 + r])
        logs = jnp.sum(obuf[r, :, :, 512:].astype(F32), axis=2, keepdims=True)
        top = jnp.max(logs, axis=0, keepdims=True)
        factor = jnp.exp(logs - top)
        numer = jnp.sum(factor * obuf[r, :, :, :512].astype(F32), axis=0)
        latents.append(numer / jnp.sum(factor, axis=0))
    latent = jnp.concatenate(latents, axis=0).astype(BF)
    r8, c16 = iota((8, 16), 0), iota((8, 16), 1)
    halves = [None, None]
    for h in range(4):
        pick = (r8 // 4 == h // 2) & (c16 == 4 * lax.rem(r8, 4) + h)
        rows = dot(jnp.where(pick, 1.0, 0.0).astype(BF), latent).astype(BF)
        val = dot(rows, wuv[h])
        halves[h % 2] = val if halves[h % 2] is None else halves[h % 2] + val
    vrow = jnp.concatenate(halves, axis=1).astype(BF)
    pl.semaphore_wait(greet.at[1], len(near_z))
    vs[...] = vrow
    vbuf[0] = vrow
    for s in ZFAR:
        pos = ZORD.index(NZ - s)
        remote(
            vs, vbuf.at[pos], snd.at[3], rcv.at[3 if pos < 7 else 9 if pos < 11 else 16],
            (lax.rem(z + s, NZ), c),
        ).start()
    sent(3, vbuf.at[pl.ds(0, 15)])

    wait("wo")
    for lo, n, sem in ((0, 7, 3), (7, 4, 9), (11, 5, 16)):
        own_block = 1 if lo == 0 else 0
        drain(vbuf.at[pl.ds(lo + own_block, n - own_block)], rcv.at[sem])
        vals = vbuf[lo : lo + n].astype(F32).reshape(8 * n, 256).astype(BF)
        y0 = dot_t(vals, wo[:, :256])
        y1 = dot_t(vals, wo[:, 256:])
        y = (y0 + pltpu.roll(y1, 8 * n - 4, 0)).reshape(n, 8, 448)
        fs[lo : lo + n, 0] = y[:, 0:2]
        fs[lo : lo + n, 1] = y[:, 2:4]
        for pos in range(lo, lo + n):
            for k in range(2):
                dst = 2 * lax.rem(z + ZORD[pos], NZ) + k

                @pl.when(dst != c)
                def _():
                    remote(
                        fs.at[pos, k], fbuf.at[c], snd.at[4], rcv.at[4], (z, dst)
                    ).start()

                @pl.when(dst == c)
                def _():
                    fbuf[c] = fs[pos, k]
    sent(4, fbuf.at[pl.ds(0, 31)])

    wait("res")
    drain(fbuf.at[pl.ds(0, 31)], rcv.at[4])
    mid = (jnp.sum(fbuf[...], axis=0) + res[...].astype(F32)).astype(BF)
    gs[...] = mid
    for s in ZFAR:
        near = [(0 - (s + k) // 2) % 8 in PAIRS[0] for k in range(2)]
        sem = 5 if all(near) else 12
        if any(near) and not all(near):
            even = lax.rem(z, 2) == 0
            sem = jnp.where(even, 5 if near[0] else 12, 5 if near[1] else 12)
        remote(
            gs, gbuf.at[z], snd.at[5], rcv.at[sem], (lax.rem(z + s, NZ), c)
        ).start()
    gbuf[z] = mid
    sent(5, gbuf.at[pl.ds(0, 15)])

    wait("wd", "wd2")
    for k in range(2):
        @pl.when(core == k)
        def _():
            for i in range(NCHIP):
                at = 448 * i + 224 * k
                wdp[i, :, :224] = wd[:, at : at + 224]

    lane_w = iota((8, 128), 1)
    sq = jnp.zeros((8, 1), F32)
    arrival = [jnp.where(seat < 8, 6, 14), jnp.where(seat < 8, 13, 15)]
    for far in range(2):
        if far == 0:
            drain(gbuf.at[pl.ds(0, 7)], rcv.at[5])
        else:
            drain(gbuf.at[pl.ds(0, 8)], rcv.at[12])
        for j in range(4):
            for b in range(2):
                mid8[far, 2 * j : 2 * j + 2, 448 * b : 448 * b + 448] = gbuf[
                    2 * pair(far, j) + b
                ].astype(F32)
        m = mid8[far]
        sq = sq + jnp.sum(m * m, axis=1, keepdims=True)
        gained = (m * gain8[far]).astype(BF)
        if far == 0:
            src, dst, i = xs, xbuf, 6
        else:
            sq = sq + pltpu.roll(sq, 2, 0)
            sq = sq + pltpu.roll(sq, 4, 0)
            norm = lax.rsqrt(sq * (1.0 / 7168.0) + EPS)
            src, dst, i = xs2, xbuf2, 10
            hi = norm.astype(BF).astype(F32)
            mi = (norm - hi).astype(BF).astype(F32)
            tail = jnp.where(
                lane_w == 0,
                hi,
                jnp.where(lane_w == 1, mi, jnp.where(lane_w == 2, norm - hi - mi, 0.0)),
            ).astype(BF)
            gained = jnp.concatenate([gained, tail], axis=1)
        src[...] = gained
        for s in FAR:
            remote(
                src, dst.at[seat], snd.at[i], rcv.at[arrival[far]],
                (z, chip_at(s) * 2 + core),
            ).start()
        dst[seat] = gained
        sent(i, dst.at[pl.ds(0, 15)])

    @pl.when(chip == z)
    def _():
        for far in range(2):
            for j in range(4):
                for d in range(4):
                    mids[4 * pair(far, j) + d] = mid8[
                        far, 2 * j : 2 * j + 2, 224 * d : 224 * d + 224
                    ]

        @pl.loop(1, NC)
        def _(s):
            dst = lax.rem(c + s, NC)
            remote(
                mids.at[dst], midbuf.at[core], snd.at[9], rcv.at[10], (z, dst)
            ).start()

        midbuf[core] = mids[c]

    wait("wg", "wu", "wg2", "wu2")
    row_j = lax.rem(iota((64, 256), 0), 8) // 2

    def arrived(buf, part, sem):
        mine = seat // 8 == part

        @pl.when(mine)
        def _():
            drain(buf.at[pl.ds(8 * part, 7)], sem)

        @pl.when(jnp.logical_not(mine))
        def _():
            drain(buf.at[pl.ds(8 * part, 8)], sem)

    def project(x, far):
        total = jnp.zeros((64, 256), F32)
        for j in range(4):
            at = pl.multiple_of(896 * pair(far, j), 128)
            total = total + jnp.where(row_j == j, dot_t(x, gu[:, pl.ds(at, 896)]), 0.0)
        return total

    keep = lax.rem(iota((64, 128), 0), 8) < 2
    r16, c64 = iota((16, 64), 0), iota((16, 64), 1)
    squeeze = jnp.where(c64 == 8 * (r16 // 2) + lax.rem(r16, 2), 1.0, 0.0).astype(BF)
    order = FAR + (0,)
    for part in range(2):
        arrived(xbuf, part, rcv.at[6 if part == 0 else 14])
        x = xbuf[8 * part : 8 * part + 8].astype(F32).reshape(64, 896).astype(BF)
        both = project(x, 0)
        arrived(xbuf2, part, rcv.at[13 if part == 0 else 15])
        x = xbuf2[8 * part : 8 * part + 8].astype(F32).reshape(64, 1024)
        norm = jnp.sum(x[:, 896:], axis=1, keepdims=True)
        both = both + project(x[:, :896].astype(BF), 1)
        both = both + pltpu.roll(both, 62, 0)
        both = (both + pltpu.roll(both, 60, 0)) * norm
        gate, up = both[:, :128], both[:, 128:]
        hidden = gate / (1.0 + jnp.exp(-gate)) * up * coefs[64 * part : 64 * part + 64]
        hidden = jnp.where(keep, hidden, 0.0).astype(BF)
        short = dot(squeeze, hidden).astype(BF)
        hs[part] = short
        twin(4 * part, "hidden%d" % part, hs.at[part], hb.at[part, core])
        hb[part, core] = short
        wait("hidden%d" % part)
        short = hb[part].reshape(32, 128)
        for lo in range(0, NCHIP, 8):
            for s in order[lo : lo + 8]:
                isend[part, s] = dot(short, wdp[chip_at(s)])[:, :224].astype(BF)
            for s in order[lo : lo + 8]:
                if s:
                    remote(
                        isend.at[part, s], ibuf.at[part, back(s)],
                        snd.at[7 if part == 0 else 11], rcv.at[7 if part == 0 else 17],
                        (z, chip_at(s) * 2 + core),
                    ).start()
        ibuf[part, 0] = isend[part, 0]
        sent(7 if part == 0 else 11, ibuf.at[part, pl.ds(0, 15)])

    for part, seats in enumerate(((4, 3, 5, 2, 6, 1, 7, 0), (8, 9, 15, 10, 14, 11, 13))):
        drain(ibuf.at[part, pl.ds(1, 15)], rcv.at[7 if part == 0 else 17])
        acc = jnp.sum(ibuf[part].astype(F32), axis=0)
        for i in range(8):
            for k in range(2):
                at = 16 * k + 2 * i
                js[8 * part + i, 2 * k : 2 * k + 2] = acc[at : at + 2]
        for i in seats:
            remote(
                js.at[i], jbuf.at[z], snd.at[8], rcv.at[8], (lax.rem(z + 4 + i, NZ), c)
            ).start()
    jbuf[z] = js[12]
    drain(jbuf.at[pl.ds(0, 15)], rcv.at[8])
    last = jnp.sum(jbuf[...], axis=0)

    @pl.when(chip == z)
    def _():
        drain(midbuf.at[0], rcv.at[10])
        drain(mids.at[pl.ds(0, 31)], snd.at[9])

    @pl.when(chip != z)
    def _():
        drain(midbuf, rcv.at[10])

    mid = jnp.concatenate([midbuf[0], midbuf[1]], axis=0)
    out_ref[...] = (last + mid).astype(BF)
    sent(8, jbuf.at[pl.ds(0, 15)])
    wait(*list(todo))


def local(
    residual, query, latent_cache, lengths, w_uv, w_o, norm_gain, routes, route_weight,
    w_gate, w_up, w_down,
):
    hbm = pl.BlockSpec(memory_space=pltpu.HBM)
    vmem = pl.BlockSpec(memory_space=pltpu.VMEM)
    V = pltpu.VMEM
    D = pltpu.SemaphoreType.DMA
    return pl.pallas_call(
        body,
        out_shape=jax.ShapeDtypeStruct((4, 224), BF),
        in_specs=[hbm] * 12,
        out_specs=vmem,
        scratch_shapes=[
            pltpu.SMEM((2,), jnp.int32),
            V((4, 4, 576), BF),
            V((2, 576, 1024), BF),
            V((4, 512, 128), BF),
            V((448, 512), BF),
            V((2, 448), BF),
            V((56, 128), BF),
            V((4, 64), jnp.int32),
            V((4, 64), F32),
            V((8, 2, 896), F32),
            V((2, 8, 896), F32),
            V((256, 7168), BF),
            V((128, 7168), BF),
            V((16, 128, 256), BF),
            V((2, 8, 576), BF),
            V((2, 16, 8, 576), BF),
            V((2, 16, 8, 640), BF),
            V((2, 16, 8, 640), BF),
            V((8, 256), BF),
            V((16, 8, 256), BF),
            V((16, 2, 2, 448), F32),
            V((32, 2, 448), F32),
            V((2, 448), BF),
            V((16, 2, 448), BF),
            V((2, 8, 896), F32),
            V((32, 2, 224), F32),
            V((2, 2, 224), F32),
            V((8, 896), BF),
            V((8, 1024), BF),
            V((16, 8, 896), BF),
            V((16, 8, 1024), BF),
            V((2, 16, 128), BF),
            V((2, 2, 16, 128), BF),
            V((2, 16, 32, 224), BF),
            V((2, 16, 32, 224), BF),
            V((16, 4, 224), F32),
            V((16, 4, 224), F32),
            D((13,)),
            D((7,)),
            D((7,)),
            D((12,)),
            D((18,)),
            pltpu.SemaphoreType.REGULAR((2,)),
        ],
        compiler_params=pltpu.CompilerParams(
            collective_id=0, has_side_effects=True, vmem_limit_bytes=48 << 20
        ),
        name="decode_layer",
    )(
        *[
            pltpu.with_memory_space_constraint(x, pltpu.HBM)
            for x in (
                lengths, query, jnp.swapaxes(latent_cache, 1, 2), w_uv, w_o.T, residual,
                norm_gain.reshape(56, 128), routes.T, route_weight.T,
                w_gate, w_up, w_down,
            )
        ],
    )


def solution(mesh):
    in_specs = (
        P("ctx", "req"),
        P("req", "ctx", None),
        P("req", "ctx", None),
        P("req"),
        P("ctx", None, None),
        P("ctx", "req"),
        P(),
        P(),
        P(),
        P("req", "ctx", None),
        P("req", "ctx", None),
        P("req", "ctx", None),
    )
    return jax.shard_map(
        local, mesh=mesh, in_specs=in_specs, out_specs=P("req", "ctx"), check_vma=False
    )
```

```python
import jax
import jax.numpy as jnp
from jax import lax
from jax.experimental import pallas as pl
from jax.experimental.pallas import tpu as pltpu
from jax.sharding import PartitionSpec as P

MESH = pl.DeviceIdType.MESH
SCALE = 192.0 ** (-0.5)
NEG = -1e30
EPS = 1e-06
BF = jnp.bfloat16
F32 = jnp.float32
NZ = 16
NC = 32
NCHIP = 16
FAR = (10, 2, 8, 9, 11, 6, 14, 1, 3, 4, 12, 5, 7, 13, 15)
ZORD = (0, 1, 15, 2, 14, 3, 13, 4, 12, 5, 11, 6, 10, 7, 9, 8)
PAIRS = ((0, 1, 7, 2), (6, 3, 5, 4))
ZFAR = (8, 7, 9, 6, 10, 5, 11, 4, 12, 3, 13, 2, 14, 1, 15)


def dot(a, b):
    return jnp.dot(a, b, preferred_element_type=F32)


def dot_t(a, b):
    return lax.dot_general(a, b, (((1,), (1,)), ((), ())), preferred_element_type=F32)


def iota(shape, axis):
    return lax.broadcasted_iota(jnp.int32, shape, axis)


def body(
    lens_hbm, q_hbm, cache_hbm, wuv_hbm, wo_hbm, res_hbm, gain_hbm, routes_hbm, rw_hbm,
    wg_hbm, wu_hbm, wd_hbm,
    out_ref,
    lens, qin, cbuf, wuv, wo, res, gain, routes, rw, table, gain8, gu, wd, wdp,
    qs, qbuf, osend, obuf, vs, vbuf, fs, fbuf, gs, gbuf, mid8, mids, midbuf, xs, xs2, xbuf, xbuf2,
    hs, hb, isend, ibuf, js, jbuf,
    loc, sib_s, sib_r, snd, rcv, greet,
):
    z = lax.axis_index("req")
    c = lax.axis_index("ctx")
    core = lax.rem(c, 2)
    chip = c // 2
    sib = c + 1 - 2 * core

    def chip_at(s):
        x = lax.rem(chip // 4 + s // 4, 4)
        y = lax.rem(lax.rem(chip, 4) + s % 4, 4)
        return x * 4 + y

    def back(s):
        return ((4 - s // 4) % 4) * 4 + (4 - s % 4) % 4

    barrier = pltpu.get_barrier_semaphore()
    near_z = (3, 13, 2, 14, 1, 15)
    for s in FAR:
        pl.semaphore_signal(
            barrier, inc=1, device_id=(z, chip_at(s) * 2 + core), device_id_type=MESH
        )
    for s in near_z:
        pl.semaphore_signal(
            barrier, inc=1, device_id=(lax.rem(z + s, NZ), c), device_id_type=MESH
        )
    pl.semaphore_signal(barrier, inc=1, device_id=(z, sib), device_id_type=MESH)

    def pass_on(i):
        for s in near_z:
            pl.semaphore_signal(
                greet.at[i], inc=1, device_id=(lax.rem(z + s, NZ), c), device_id_type=MESH
            )

    todo = {}

    def begin(name, copy):
        copy.start()
        todo[name] = copy.wait

    def wait(*names):
        for name in names:
            todo.pop(name)()

    def drain(ref, sem):
        pltpu.make_async_copy(ref, ref, sem).wait()

    own, other = pl.ds(0, 512), pl.ds(512, 512)
    first = pl.ds(pl.multiple_of(64 * core, 64), 64)
    second = pl.ds(pl.multiple_of(128 + 64 * core, 64), 64)
    for i, (name, src, dst) in enumerate((
        ("q", q_hbm, qin),
        ("cache0", cache_hbm.at[0], cbuf.at[0, :, own]),
        ("cache1", cache_hbm.at[1], cbuf.at[1, :, own]),
        ("gain", gain_hbm, gain),
        ("routes", routes_hbm, routes),
        ("rw", rw_hbm, rw),
        ("res", res_hbm, res),
        ("wuv", wuv_hbm, wuv),
        ("wo", wo_hbm, wo),
        ("wg", wg_hbm.at[0], gu.at[first]),
        ("wu", wu_hbm.at[0], gu.at[second]),
        ("wd", wd_hbm.at[0], wd.at[first]),
        ("lens", lens_hbm, lens),
    )):
        begin(name, pltpu.make_async_copy(src, dst, loc.at[i]))

    def remote(src, dst, send, recv, dev):
        return pltpu.make_async_remote_copy(
            src_ref=src, dst_ref=dst, send_sem=send, recv_sem=recv,
            device_id=dev, device_id_type=MESH,
        )

    def twin(i, name, src, dst):
        copy = remote(src, dst, sib_s.at[i], sib_r.at[i], (z, sib))
        copy.start()
        todo[name] = copy.wait_recv
        todo[name + "_sent"] = copy.wait_send

    def sent(i, ref):
        todo["sent%d" % i] = lambda: drain(ref, snd.at[i])

    wait("q")
    for r in range(2):
        rows = jnp.concatenate(
            [qin[2 * r].astype(F32), qin[2 * r + 1].astype(F32)], axis=0
        ).astype(BF)
        qs[r] = rows
        qbuf[r, 0] = rows
    pl.semaphore_wait(barrier, len(near_z) + NCHIP)
    for r in range(2):
        for s in FAR:
            remote(
                qs.at[r], qbuf.at[r, back(s)], snd.at[0], rcv.at[0 if r == 0 else 11],
                (z, chip_at(s) * 2 + core),
            ).start()
        twin(5 + r, "twin%d" % r, cache_hbm.at[r], cbuf.at[r, :, other])
    sent(0, qbuf.at[:, pl.ds(0, 15)])
    pass_on(0)
    twin(1, "wg2", wg_hbm.at[0], gu.at[first])
    twin(2, "wu2", wu_hbm.at[0], gu.at[second])
    twin(3, "wd2", wd_hbm.at[0], wd.at[first])

    wait("gain", "routes", "rw")
    g = gain[...].astype(F32)
    for i in range(56):
        m, j = i // 7, i % 7
        table[m, :, 128 * j : 128 * j + 128] = jnp.broadcast_to(g[i : i + 1], (2, 128))

    def pair(far, j):
        return lax.rem(z // 2 + PAIRS[far][j], 8)

    for far in range(2):
        for j in range(4):
            gain8[far, 2 * j : 2 * j + 2] = table[pair(far, j)]
    seat = lax.rem(chip - z + 28, NCHIP)
    coef = jnp.sum(jnp.where(routes[...] == z, rw[...], 0.0), axis=0, keepdims=True)
    row = iota((128, 64), 0)
    token = 4 * lax.rem(row // 8 + z + 4, NCHIP) + 2 * core + lax.rem(row, 2)
    pick = (token == iota((128, 64), 1)) & (lax.rem(row, 8) < 2)
    coefs = jnp.sum(jnp.where(pick, coef, 0.0), axis=1, keepdims=True)

    wait("lens")
    row_k = lax.rem(iota((128, 1024), 0) // 4, 2)
    lane_p = iota((128, 1024), 1)
    place = jnp.where(lane_p < 512, c * 512 + lane_p, sib * 512 + lane_p - 512)
    lane_e = iota((128, 128), 1)
    for r in range(2):
        wait("cache%d" % r, "twin%d" % r)
        drain(qbuf.at[r, pl.ds(1, 15)], rcv.at[0 if r == 0 else 11])
        ql = qbuf[r].astype(F32).reshape(128, 576).astype(BF)
        see = place <= lens[r] - 2 + row_k
        score = jnp.where(see, dot(ql, cbuf[r]) * SCALE, NEG)
        peak = jnp.max(score, axis=1, keepdims=True)
        peak = jnp.where(peak > 0.5 * NEG, peak, 0.0)
        raised = jnp.exp(score - peak)
        total = jnp.sum(raised, axis=1, keepdims=True)
        mixed = dot_t(raised.astype(BF), cbuf[r, :512])
        filled = total > 0.0
        safe = jnp.where(filled, total, 1.0)
        part = jnp.where(filled, mixed / safe, 0.0)
        log = jnp.where(filled, peak + jnp.log(safe), NEG)
        hi = log.astype(BF).astype(F32)
        mi = (log - hi).astype(BF).astype(F32)
        lo = log - hi - mi
        tail = jnp.where(
            lane_e == 0, hi, jnp.where(lane_e == 1, mi, jnp.where(lane_e == 2, lo, 0.0))
        )
        osend[r, :, :, :512] = part.reshape(16, 8, 512).astype(BF)
        osend[r, :, :, 512:] = tail.reshape(16, 8, 128).astype(BF)
        for s in FAR:
            remote(
                osend.at[r, s], obuf.at[r, back(s)], snd.at[1 + r], rcv.at[1 + r],
                (z, chip_at(s) * 2 + core),
            ).start()
        obuf[r, 0] = osend[r, 0]
        sent(1 + r, obuf.at[r, pl.ds(0, 15)])

    pl.semaphore_wait(greet.at[0], len(near_z))
    pass_on(1)
    wait("wuv")
    latents = []
    for r in range(2):
        drain(obuf.at[r, pl.ds(1, 15)], rcv.at[1 + r])
        logs = jnp.sum(obuf[r, :, :, 512:].astype(F32), axis=2, keepdims=True)
        top = jnp.max(logs, axis=0, keepdims=True)
        factor = jnp.exp(logs - top)
        numer = jnp.sum(factor * obuf[r, :, :, :512].astype(F32), axis=0)
        latents.append(numer / jnp.sum(factor, axis=0))
    latent = jnp.concatenate(latents, axis=0).astype(BF)
    r8, c16 = iota((8, 16), 0), iota((8, 16), 1)
    halves = [None, None]
    for h in range(4):
        pick = (r8 // 4 == h // 2) & (c16 == 4 * lax.rem(r8, 4) + h)
        rows = dot(jnp.where(pick, 1.0, 0.0).astype(BF), latent).astype(BF)
        val = dot(rows, wuv[h])
        halves[h % 2] = val if halves[h % 2] is None else halves[h % 2] + val
    vrow = jnp.concatenate(halves, axis=1).astype(BF)
    pl.semaphore_wait(greet.at[1], len(near_z))
    vs[...] = vrow
    vbuf[0] = vrow
    for s in ZFAR:
        pos = ZORD.index(NZ - s)
        remote(
            vs, vbuf.at[pos], snd.at[3], rcv.at[3 if pos < 7 else 9 if pos < 11 else 16],
            (lax.rem(z + s, NZ), c),
        ).start()
    sent(3, vbuf.at[pl.ds(0, 15)])

    wait("wo")
    for lo, n, sem in ((0, 7, 3), (7, 4, 9), (11, 5, 16)):
        own_block = 1 if lo == 0 else 0
        drain(vbuf.at[pl.ds(lo + own_block, n - own_block)], rcv.at[sem])
        vals = vbuf[lo : lo + n].astype(F32).reshape(8 * n, 256).astype(BF)
        y0 = dot_t(vals, wo[:, :256])
        y1 = dot_t(vals, wo[:, 256:])
        y = (y0 + pltpu.roll(y1, 8 * n - 4, 0)).reshape(n, 8, 448)
        fs[lo : lo + n, 0] = y[:, 0:2]
        fs[lo : lo + n, 1] = y[:, 2:4]
        for pos in range(lo, lo + n):
            for k in range(2):
                dst = 2 * lax.rem(z + ZORD[pos], NZ) + k

                @pl.when(dst != c)
                def _():
                    remote(
                        fs.at[pos, k], fbuf.at[c], snd.at[4], rcv.at[4], (z, dst)
                    ).start()

                @pl.when(dst == c)
                def _():
                    fbuf[c] = fs[pos, k]
    sent(4, fbuf.at[pl.ds(0, 31)])

    wait("res")
    drain(fbuf.at[pl.ds(0, 31)], rcv.at[4])
    mid = (jnp.sum(fbuf[...], axis=0) + res[...].astype(F32)).astype(BF)
    gs[...] = mid
    for s in ZFAR:
        near = [(0 - (s + k) // 2) % 8 in PAIRS[0] for k in range(2)]
        sem = 5 if all(near) else 12
        if any(near) and not all(near):
            even = lax.rem(z, 2) == 0
            sem = jnp.where(even, 5 if near[0] else 12, 5 if near[1] else 12)
        remote(
            gs, gbuf.at[z], snd.at[5], rcv.at[sem], (lax.rem(z + s, NZ), c)
        ).start()
    gbuf[z] = mid
    sent(5, gbuf.at[pl.ds(0, 15)])

    wait("wd", "wd2")
    for k in range(2):
        @pl.when(core == k)
        def _():
            for i in range(NCHIP):
                at = 448 * i + 224 * k
                wdp[i, :, :224] = wd[:, at : at + 224]

    lane_w = iota((8, 128), 1)
    sq = jnp.zeros((8, 1), F32)
    arrival = [jnp.where(seat < 8, 6, 14), jnp.where(seat < 8, 13, 15)]
    for far in range(2):
        if far == 0:
            drain(gbuf.at[pl.ds(0, 7)], rcv.at[5])
        else:
            drain(gbuf.at[pl.ds(0, 8)], rcv.at[12])
        for j in range(4):
            for b in range(2):
                mid8[far, 2 * j : 2 * j + 2, 448 * b : 448 * b + 448] = gbuf[
                    2 * pair(far, j) + b
                ].astype(F32)
        m = mid8[far]
        sq = sq + jnp.sum(m * m, axis=1, keepdims=True)
        gained = (m * gain8[far]).astype(BF)
        if far == 0:
            src, dst, i = xs, xbuf, 6
        else:
            sq = sq + pltpu.roll(sq, 2, 0)
            sq = sq + pltpu.roll(sq, 4, 0)
            norm = lax.rsqrt(sq * (1.0 / 7168.0) + EPS)
            src, dst, i = xs2, xbuf2, 10
            hi = norm.astype(BF).astype(F32)
            mi = (norm - hi).astype(BF).astype(F32)
            tail = jnp.where(
                lane_w == 0,
                hi,
                jnp.where(lane_w == 1, mi, jnp.where(lane_w == 2, norm - hi - mi, 0.0)),
            ).astype(BF)
            gained = jnp.concatenate([gained, tail], axis=1)
        src[...] = gained
        for s in FAR:
            remote(
                src, dst.at[seat], snd.at[i], rcv.at[arrival[far]],
                (z, chip_at(s) * 2 + core),
            ).start()
        dst[seat] = gained
        sent(i, dst.at[pl.ds(0, 15)])

    @pl.when(chip == z)
    def _():
        for far in range(2):
            for j in range(4):
                for d in range(4):
                    mids[4 * pair(far, j) + d] = mid8[
                        far, 2 * j : 2 * j + 2, 224 * d : 224 * d + 224
                    ]

        @pl.loop(1, NC)
        def _(s):
            dst = lax.rem(c + s, NC)
            remote(
                mids.at[dst], midbuf.at[core], snd.at[9], rcv.at[10], (z, dst)
            ).start()

        midbuf[core] = mids[c]

    wait("wg", "wu", "wg2", "wu2")
    row_j = lax.rem(iota((64, 256), 0), 8) // 2

    def arrived(buf, part, sem):
        mine = seat // 8 == part

        @pl.when(mine)
        def _():
            drain(buf.at[pl.ds(8 * part, 7)], sem)

        @pl.when(jnp.logical_not(mine))
        def _():
            drain(buf.at[pl.ds(8 * part, 8)], sem)

    def project(x, far):
        total = jnp.zeros((64, 256), F32)
        for j in range(4):
            at = pl.multiple_of(896 * pair(far, j), 128)
            total = total + jnp.where(row_j == j, dot_t(x, gu[:, pl.ds(at, 896)]), 0.0)
        return total

    keep = lax.rem(iota((64, 128), 0), 8) < 2
    r16, c64 = iota((16, 64), 0), iota((16, 64), 1)
    squeeze = jnp.where(c64 == 8 * (r16 // 2) + lax.rem(r16, 2), 1.0, 0.0).astype(BF)
    order = FAR + (0,)
    for part in range(2):
        arrived(xbuf, part, rcv.at[6 if part == 0 else 14])
        x = xbuf[8 * part : 8 * part + 8].astype(F32).reshape(64, 896).astype(BF)
        both = project(x, 0)
        arrived(xbuf2, part, rcv.at[13 if part == 0 else 15])
        x = xbuf2[8 * part : 8 * part + 8].astype(F32).reshape(64, 1024)
        norm = jnp.sum(x[:, 896:], axis=1, keepdims=True)
        both = both + project(x[:, :896].astype(BF), 1)
        both = both + pltpu.roll(both, 62, 0)
        both = (both + pltpu.roll(both, 60, 0)) * norm
        gate, up = both[:, :128], both[:, 128:]
        hidden = gate / (1.0 + jnp.exp(-gate)) * up * coefs[64 * part : 64 * part + 64]
        hidden = jnp.where(keep, hidden, 0.0).astype(BF)
        short = dot(squeeze, hidden).astype(BF)
        hs[part] = short
        twin(4 * part, "hidden%d" % part, hs.at[part], hb.at[part, core])
        hb[part, core] = short
        wait("hidden%d" % part)
        short = hb[part].reshape(32, 128)
        for lo in range(0, NCHIP, 8):
            for s in order[lo : lo + 8]:
                isend[part, s] = dot(short, wdp[chip_at(s)])[:, :224].astype(BF)
            for s in order[lo : lo + 8]:
                if s:
                    remote(
                        isend.at[part, s], ibuf.at[part, back(s)],
                        snd.at[7 if part == 0 else 11], rcv.at[7 if part == 0 else 17],
                        (z, chip_at(s) * 2 + core),
                    ).start()
        ibuf[part, 0] = isend[part, 0]
        sent(7 if part == 0 else 11, ibuf.at[part, pl.ds(0, 15)])

    for part, seats in enumerate(((4, 3, 5, 2, 6, 1, 7, 0), (8, 9, 15, 10, 14, 11, 13))):
        drain(ibuf.at[part, pl.ds(1, 15)], rcv.at[7 if part == 0 else 17])
        acc = jnp.sum(ibuf[part].astype(F32), axis=0)
        for i in range(8):
            for k in range(2):
                at = 16 * k + 2 * i
                js[8 * part + i, 2 * k : 2 * k + 2] = acc[at : at + 2]
        for i in seats:
            remote(
                js.at[i], jbuf.at[z], snd.at[8], rcv.at[8], (lax.rem(z + 4 + i, NZ), c)
            ).start()
    jbuf[z] = js[12]
    drain(jbuf.at[pl.ds(0, 15)], rcv.at[8])
    last = jnp.sum(jbuf[...], axis=0)

    @pl.when(chip == z)
    def _():
        drain(midbuf.at[0], rcv.at[10])
        drain(mids.at[pl.ds(0, 31)], snd.at[9])

    @pl.when(chip != z)
    def _():
        drain(midbuf, rcv.at[10])

    mid = jnp.concatenate([midbuf[0], midbuf[1]], axis=0)
    out_ref[...] = (last + mid).astype(BF)
    sent(8, jbuf.at[pl.ds(0, 15)])
    wait(*list(todo))


def local(
    residual, query, latent_cache, lengths, w_uv, w_o, norm_gain, routes, route_weight,
    w_gate, w_up, w_down,
):
    hbm = pl.BlockSpec(memory_space=pltpu.HBM)
    vmem = pl.BlockSpec(memory_space=pltpu.VMEM)
    V = pltpu.VMEM
    D = pltpu.SemaphoreType.DMA
    return pl.pallas_call(
        body,
        out_shape=jax.ShapeDtypeStruct((4, 224), BF),
        in_specs=[hbm] * 12,
        out_specs=vmem,
        scratch_shapes=[
            pltpu.SMEM((2,), jnp.int32),
            V((4, 4, 576), BF),
            V((2, 576, 1024), BF),
            V((4, 512, 128), BF),
            V((448, 512), BF),
            V((2, 448), BF),
            V((56, 128), BF),
            V((4, 64), jnp.int32),
            V((4, 64), F32),
            V((8, 2, 896), F32),
            V((2, 8, 896), F32),
            V((256, 7168), BF),
            V((128, 7168), BF),
            V((16, 128, 256), BF),
            V((2, 8, 576), BF),
            V((2, 16, 8, 576), BF),
            V((2, 16, 8, 640), BF),
            V((2, 16, 8, 640), BF),
            V((8, 256), BF),
            V((16, 8, 256), BF),
            V((16, 2, 2, 448), F32),
            V((32, 2, 448), F32),
            V((2, 448), BF),
            V((16, 2, 448), BF),
            V((2, 8, 896), F32),
            V((32, 2, 224), F32),
            V((2, 2, 224), F32),
            V((8, 896), BF),
            V((8, 1024), BF),
            V((16, 8, 896), BF),
            V((16, 8, 1024), BF),
            V((2, 16, 128), BF),
            V((2, 2, 16, 128), BF),
            V((2, 16, 32, 224), BF),
            V((2, 16, 32, 224), BF),
            V((16, 4, 224), F32),
            V((16, 4, 224), F32),
            D((13,)),
            D((7,)),
            D((7,)),
            D((12,)),
            D((18,)),
            pltpu.SemaphoreType.REGULAR((2,)),
        ],
        compiler_params=pltpu.CompilerParams(
            collective_id=0, has_side_effects=True, vmem_limit_bytes=48 << 20
        ),
        name="decode_layer",
    )(
        *[
            pltpu.with_memory_space_constraint(x, pltpu.HBM)
            for x in (
                lengths, query, jnp.swapaxes(latent_cache, 1, 2), w_uv, w_o.T, residual,
                norm_gain.reshape(56, 128), routes.T, route_weight.T,
                w_gate, w_up, w_down,
            )
        ],
    )


def solution(mesh):
    in_specs = (
        P("ctx", "req"),
        P("req", "ctx", None),
        P("req", "ctx", None),
        P("req"),
        P("ctx", None, None),
        P("ctx", "req"),
        P(),
        P(),
        P(),
        P("req", "ctx", None),
        P("req", "ctx", None),
        P("req", "ctx", None),
    )
    return jax.shard_map(
        local, mesh=mesh, in_specs=in_specs, out_specs=P("req", "ctx"), check_vma=False
    )
```
